128 devices in a mesh: ctx: 16 (over z, y), fsdp: 8 (over x, core).
Axes of the slice: x: 4, y: 4, z: 4, core: 2. Of those that a mesh axis runs over, the one named last changes fastest.
Arguments:
- query_rows: bfloat16 [16384, 8192], P(('fsdp', 'ctx')), may hold values from -6 to 6
- key_rows: bfloat16 [16384, 1024], P(('fsdp', 'ctx')), may hold values from -6 to 6
- value_rows: bfloat16 [16384, 1024], P(('fsdp', 'ctx')), may hold values from -6 to 6
- grad_out: bfloat16 [16384, 8192], P(('fsdp', 'ctx')), may hold values from -384 to 384
- query_map: bfloat16 [64, 128, 64], P('ctx', 'fsdp'), may hold values from -1.5 to 1.5
- key_map: bfloat16 [64, 128, 64], P('ctx', 'fsdp'), may hold values from -1.5 to 1.5
- prefix_state: float32 [64, 128, 128], P('ctx'), may hold values from -24 to 24
- prefix_norm: float32 [64, 128], P('ctx'), may hold values from 16 to 256
Outputs:
- grad_queries: bfloat16 [16384, 8192], P(('fsdp', 'ctx'))
- grad_keys: bfloat16 [16384, 1024], P(('fsdp', 'ctx'))
- grad_values: bfloat16 [16384, 1024], P(('fsdp', 'ctx'))
- grad_query_map: float32 [64, 128, 64], P('ctx', 'fsdp')
- grad_key_map: float32 [64, 128, 64], P('ctx', 'fsdp')
- grad_prefix_state: float32 [64, 128, 128], P('ctx', 'fsdp')
The draws below stay inside these ranges and needn't reach their ends.
All inputs are finite; a program needn't handle non-finite values.
Results may differ from the reference program's by a relative error of at most 0.014.
The reference program's roundings to bfloat16 on the way (of `query_logits`, `key_logits`, `state_low`, `scores_low`, `scaled_low`, `dscores` and `suffix_low`) count: a program that leaves them out, or rounds other values in their place, can miss the bound.
Values may be sent and summed in bfloat16 or wider, within the bound.
A program may use at most 128 MiB of HBM per device.

```python
import math
import jax
import jax.numpy as jnp
from jax import lax

H = 64
KVH = 8
HD = 128
FH = 64
BLK = 512
GROUP = 8
TOKENS = 16384


def levels(own_key, dims, cuts, smallest, largest):
    factor_of, own = 1.0, jax.random.fold_in(own_key, 6)
    for axis_at, blocks in cuts:
        heights = jnp.exp(jax.random.uniform(jax.random.fold_in(own, axis_at), (blocks,), jnp.float32, smallest / len(cuts), largest / len(cuts)))
        factor_of = factor_of * jnp.repeat(heights, dims[axis_at] // blocks).reshape([-1 if axis == axis_at else 1 for axis in range(len(dims))])
    return factor_of


def normal_values(key, shape, width, most, shards=(), kind=jnp.bfloat16):
    gain = levels(key, shape, shards, -0.22, 0.18) if shards else 1.0
    result = jax.random.normal(key, shape, jnp.float32) * width * gain
    return jnp.minimum(jnp.maximum(result, -most), most).astype(kind)


def setup_inputs(seed: int = 0) -> dict:
    keys = jax.random.split(jax.random.key(seed), 9)
    return {
        "query_rows": normal_values(keys[0], (TOKENS, H * HD), 1.0, 6.0, ((0, 128),)),
        "key_rows": normal_values(keys[1], (TOKENS, KVH * HD), 1.0, 6.0, ((0, 128),)),
        "value_rows": normal_values(keys[2], (TOKENS, KVH * HD), 1.0, 6.0, ((0, 128),)),
        "grad_out": normal_values(keys[3], (TOKENS, H * HD), (HD // 2), 384.0, ((0, 128),)),
        "query_map": normal_values(keys[4], (H, HD, FH), (HD // 8) ** -0.5, 1.5, ((0, 16), (1, 8))),
        "key_map": normal_values(keys[5], (H, HD, FH), (HD // 8) ** -0.5, 1.5, ((0, 16), (1, 8))),
        "prefix_state": normal_values(keys[6], (H, 2 * FH, HD), 4.0, 24.0, ((0, 16),), jnp.float32),
        "prefix_norm": jnp.clip(jnp.exp(math.log(256.0) - 2.7725887 * jax.random.uniform(keys[7], (H, 2 * FH), jnp.float32) ** levels(keys[7], (H, 2 * FH), ((0, 16),), -0.2, 0.2)), 16.0, 256.0),
    }


precise = lax.Precision.HIGHEST


def round_low(array):
    return lax.optimization_barrier(array.astype(jnp.bfloat16))


def to_wide(array):
    return array.astype(jnp.float32)


def feature_pair(logits):
    widened = logits.astype(jnp.float32)
    upper_exp = jnp.exp(widened)
    lower_exp = jnp.exp(-widened)
    return upper_exp / jnp.sum(upper_exp, axis=-1, keepdims=True), lower_exp / jnp.sum(lower_exp, axis=-1, keepdims=True)


def feature_back(positive, negative, upstream):
    half_width = positive.shape[-1]
    first_half = upstream[..., :half_width]
    second_half = upstream[..., half_width:]
    first_term = positive * (first_half - jnp.sum(positive * first_half, axis=-1, keepdims=True))
    second_term = negative * (second_half - jnp.sum(negative * second_half, axis=-1, keepdims=True))
    return first_term - second_term


def causal_mask(length):
    position = jnp.arange(length)
    return (position[:, None] >= position[None, :]).astype(jnp.float32)


def recompute(state_sum, norm_sum, queries, key_part, value_part, grad_part, query_map, key_map):
    key_wide = jnp.repeat(key_part, GROUP, axis=1)
    value_wide = jnp.repeat(value_part, GROUP, axis=1)
    query_logits = round_low(jnp.einsum("thd,hdf->thf", to_wide(queries), to_wide(query_map)))
    key_logits = round_low(jnp.einsum("thd,hdf->thf", to_wide(key_wide), to_wide(key_map)))
    query_pos, query_neg = feature_pair(query_logits)
    key_pos, key_neg = feature_pair(key_logits)
    query_feat = to_wide(round_low(jnp.concatenate((query_pos, query_neg), axis=-1)))
    key_feat = to_wide(round_low(jnp.concatenate((key_pos, key_neg), axis=-1)))
    state_low = to_wide(round_low(state_sum))
    scores = jnp.einsum("thf,shf->hts", query_feat, key_feat) * causal_mask(BLK)
    scores_low = to_wide(round_low(scores))
    numerator = jnp.einsum("thf,hfd->thd", query_feat, state_low) + jnp.einsum("hts,shd->thd", scores_low, to_wide(value_wide))
    denominator = jnp.einsum("thf,hf->th", query_feat, norm_sum, precision=precise) + jnp.sum(scores, axis=-1).T
    attended = numerator / denominator[..., None]
    scaled = to_wide(grad_part) / denominator[..., None]
    scaled_low = to_wide(round_low(scaled))
    norm_grad = -jnp.sum(scaled * attended, axis=-1)
    return (key_wide, value_wide, query_pos, query_neg, key_pos, key_neg, query_feat, key_feat, state_low, scores_low, scaled_low, norm_grad)


def advance(state_sum, norm_sum, key_feat, value_wide):
    new_state = state_sum + jnp.einsum("shf,shd->hfd", key_feat, to_wide(value_wide))
    new_norm = norm_sum + jnp.sum(key_feat, axis=0)
    return new_state, new_norm


def reference(query_rows, key_rows, value_rows, grad_out, query_map, key_map, prefix_state, prefix_norm):
    blocks = TOKENS // BLK
    block_inputs = (query_rows.reshape(blocks, BLK, H, HD), key_rows.reshape(blocks, BLK, KVH, HD), value_rows.reshape(blocks, BLK, KVH, HD), grad_out.reshape(blocks, BLK, H, HD))

    def forward_step(carried, block_items):
        state_sum, norm_sum = carried
        queries, key_part, value_part, grad_part = block_items
        pieces = recompute(state_sum, norm_sum, queries, key_part, value_part, grad_part, query_map, key_map)
        value_wide = pieces[1]
        query_feat = pieces[6]
        key_feat = pieces[7]
        scaled_low = pieces[10]
        norm_grad = pieces[11]
        suffix_part = jnp.einsum("thf,thd->hfd", query_feat, scaled_low)
        suffix_norm_part = jnp.einsum("thf,th->hf", query_feat, norm_grad, precision=precise)
        return advance(state_sum, norm_sum, key_feat, value_wide), (suffix_part, suffix_norm_part)

    final_state, (suffix_parts, suffix_norms) = lax.scan(forward_step, (prefix_state, prefix_norm), block_inputs)
    suffix_next = jnp.flip(jnp.cumsum(jnp.flip(suffix_parts, 0), axis=0), 0) - suffix_parts
    suffix_norm_next = jnp.flip(jnp.cumsum(jnp.flip(suffix_norms, 0), axis=0), 0) - suffix_norms
    mask = causal_mask(BLK)

    def backward_step(carried, block_items):
        state_sum, norm_sum, query_map_acc, key_map_acc = carried
        queries, key_part, value_part, grad_part, suffix_after, suffix_norm_after = block_items
        (key_wide, value_wide, query_pos, query_neg, key_pos, key_neg, query_feat, key_feat, state_low, scores_low, scaled_low, norm_grad) = recompute(state_sum, norm_sum, queries, key_part, value_part, grad_part, query_map, key_map)
        dscores = (jnp.einsum("thd,shd->hts", scaled_low, to_wide(value_wide)) + norm_grad.T[:, :, None]) * mask
        dscores_low = to_wide(round_low(dscores))
        suffix_low = to_wide(round_low(suffix_after))
        dfeat_query = jnp.einsum("thd,hfd->thf", scaled_low, state_low) + norm_grad[..., None] * norm_sum[None] + jnp.einsum("hts,shf->thf", dscores_low, key_feat)
        dfeat_key = jnp.einsum("hts,thf->shf", dscores_low, query_feat) + jnp.einsum("shd,hfd->shf", to_wide(value_wide), suffix_low) + suffix_norm_after[None]
        dvalue = jnp.einsum("hts,thd->shd", scores_low, scaled_low) + jnp.einsum("shf,hfd->shd", key_feat, suffix_low)
        dlog_query = to_wide(round_low(feature_back(query_pos, query_neg, dfeat_query)))
        dlog_key = to_wide(round_low(feature_back(key_pos, key_neg, dfeat_key)))
        query_grad = jnp.einsum("thf,hdf->thd", dlog_query, to_wide(query_map)).astype(jnp.bfloat16)
        key_heads_grad = jnp.einsum("shf,hdf->shd", dlog_key, to_wide(key_map))
        key_grad = jnp.sum(key_heads_grad.reshape(BLK, KVH, GROUP, HD), axis=2).astype(jnp.bfloat16)
        value_grad = jnp.sum(dvalue.reshape(BLK, KVH, GROUP, HD), axis=2).astype(jnp.bfloat16)
        query_map_acc = query_map_acc + jnp.einsum("thd,thf->hdf", to_wide(queries), dlog_query)
        key_map_acc = key_map_acc + jnp.einsum("thd,thf->hdf", to_wide(key_wide), dlog_key)
        new_state, new_norm = advance(state_sum, norm_sum, key_feat, value_wide)
        return (new_state, new_norm, query_map_acc, key_map_acc), (query_grad, key_grad, value_grad)

    start = (prefix_state, prefix_norm, jnp.zeros((H, HD, FH), jnp.float32), jnp.zeros((H, HD, FH), jnp.float32))
    finals, outputs = lax.scan(backward_step, start, block_inputs + (suffix_next, suffix_norm_next))
    grad_queries = outputs[0].reshape(TOKENS, H * HD)
    grad_keys = outputs[1].reshape(TOKENS, KVH * HD)
    grad_values = outputs[2].reshape(TOKENS, KVH * HD)
    grad_prefix_state = jnp.sum(suffix_parts, axis=0)
    return (grad_queries, grad_keys, grad_values, finals[2], finals[3], grad_prefix_state)
```

```python
import functools

import jax
import jax.numpy as jnp
from jax import lax
from jax.experimental import pallas as pl
from jax.experimental.pallas import tpu as pltpu
from jax.sharding import PartitionSpec as P

HD = 128
FH = 64
BLK = 512
EXT = 136
EXL = 144
MESH = pl.DeviceIdType.MESH
F32 = jnp.float32
BF = jnp.bfloat16


def mm(a, b, ca=1, cb=0):
    return lax.dot_general(a, b, (((ca,), (cb,)), ((), ())), preferred_element_type=F32)


def soft_pair(logits):
    wide = logits.astype(BF).astype(F32)
    up = jnp.exp(wide)
    low = jnp.exp(-wide)
    pos = up * (1.0 / jnp.sum(up, axis=0, keepdims=True))
    neg = low * (1.0 / jnp.sum(low, axis=0, keepdims=True))
    return pos, neg


def soft_back(pos, neg, up):
    one = up[:FH]
    two = up[FH:]
    first = pos * (one - jnp.sum(pos * one, axis=0, keepdims=True))
    second = neg * (two - jnp.sum(neg * two, axis=0, keepdims=True))
    return (first - second).astype(BF)


def three_rows(row, height):
    high = row.astype(BF).astype(F32)
    rest = row - high
    mid = rest.astype(BF).astype(F32)
    last = rest - mid
    at = lax.broadcasted_iota(jnp.int32, (height, row.shape[1]), 0)
    zero = jnp.zeros((height, row.shape[1]), F32)
    out = jnp.where(at == 0, high, jnp.where(at == 1, mid, jnp.where(at == 2, last, zero)))
    return out.astype(BF)


def low_ext(wide):
    return jnp.concatenate((wide[:HD].astype(BF), three_rows(wide[HD : HD + 1], 16)), axis=0)


def norm_column(low):
    tail = low[HD:EXL].astype(F32)
    row = tail[0:1] + tail[1:2] + tail[2:3]
    return jnp.transpose(jnp.broadcast_to(row, (8, HD)))[:, 0:1]


def kernel(
    maps, pext, q, g, k, v,
    oq, ok, ov, om, op,
    m1, mp, mt, qh, gh, kh, vh, vt, kf, kft, kp,
    sext, uext, rin, uin, xin, yin, pin, rout, uout, stl, sul,
    dfk, dvt, dk, gq, gmt, gm, rm, xms, xm, fms, pgs, gk, gv, acc,
    m1s, m1r, m2s, m2r, ps, pr, kvs, kvr, qgs, qgr, loc,
    ss, sr, xs, xr, bs, br, us, ur, ys, yr, cs, cr, oqs, oqr, kos, kor,
    ms, mr, ns, nr, fs, fr, gs, gr,
):
    ctx = lax.axis_index("ctx")
    fsd = lax.axis_index("fsdp")
    z = ctx // 4
    y = ctx % 4
    x = fsd // 2
    c = fsd % 2
    r = c * 4 + z

    def rdma(src, dst, ssem, rsem, dev):
        return pltpu.make_async_remote_copy(
            src_ref=src, dst_ref=dst, send_sem=ssem, recv_sem=rsem, device_id=dev, device_id_type=MESH
        )

    def await_on(ref, sem):
        pltpu.make_async_copy(ref, ref, sem).wait()

    barrier = pltpu.get_barrier_semaphore()
    for j in range(1, 16):
        pl.semaphore_signal(barrier, inc=1, device_id=((ctx + j) % 16, fsd), device_id_type=MESH)
    for j in range(1, 8):
        pl.semaphore_signal(barrier, inc=1, device_id=(ctx, (fsd + j) % 8), device_id_type=MESH)
    other = fsd + 1 - 2 * c
    for j in range(1, 16):
        pl.semaphore_signal(barrier, inc=1, device_id=((ctx + j) % 16, other), device_id_type=MESH)
    pl.semaphore_wait(barrier, 37)

    def y_dev(t):
        return (z * 4 + t, fsd)

    own_rows = pl.ds(y * 128, 128)

    def put(src, dst, ssem, rsem, dev_ctx, dev_f):
        is_me = jnp.logical_and(dev_ctx == ctx, dev_f == fsd)

        @pl.when(is_me)
        def _():
            pltpu.make_async_copy(src, dst, rsem).start()

        @pl.when(jnp.logical_not(is_me))
        def _():
            rdma(src, dst, ssem, rsem, (dev_ctx, dev_f)).start()

    def sent(src, ssem, dev_ctx, dev_f):
        is_me = jnp.logical_and(dev_ctx == ctx, dev_f == fsd)

        @pl.when(jnp.logical_not(is_me))
        def _():
            await_on(src, ssem)

    for t in range(4):
        put(maps, m1.at[pl.ds(4 * y, 4)], m1s.at[t], m1r.at[y], t * 4 + z, fsd)
    pre_ctx = (2 * (y % 2) + c) * 4 + z
    pre_f = 2 * x + y // 2
    put(pext.at[pl.ds(2 * c, 2)], pin, ps, pr, pre_ctx, pre_f)

    for n, (src, dst) in enumerate(((k, kh), (v, vh))):
        for d in range(1, 4):
            t = (y + d) % 4
            rdma(
                src.at[:, pl.ds(pl.multiple_of(t * 256, 256), 256)], dst.at[own_rows, :],
                kvs.at[n, d - 1], kvr.at[n, d - 1], y_dev(t),
            ).start()
        pltpu.make_async_copy(
            src.at[:, pl.ds(pl.multiple_of(y * 256, 256), 256)], dst.at[own_rows, :], loc.at[n]
        ).start()

    def qg_copy(i, n, d):
        src, dst = ((q, qh), (g, gh))[n]
        t = (y + d) % 4
        return rdma(
            src.at[:, pl.ds(pl.multiple_of(t * 2048 + i * 256, 256), 256)],
            dst.at[own_rows, pl.ds(pl.multiple_of(i * 256, 256), 256)],
            qgs.at[i, n, d - 1], qgr.at[i, n, d - 1], y_dev(t),
        )

    def qg_own(i, n):
        src, dst = ((q, qh), (g, gh))[n]
        return pltpu.make_async_copy(
            src.at[:, pl.ds(pl.multiple_of(y * 2048 + i * 256, 256), 256)],
            dst.at[own_rows, pl.ds(pl.multiple_of(i * 256, 256), 256)],
            loc.at[2 + n * 8 + i],
        )

    def qg_start(i, carry):
        for n in range(2):
            for d in range(1, 4):
                qg_copy(i, n, d).start()
            qg_own(i, n).start()
        return carry

    lax.fori_loop(0, 8, qg_start, 0)

    for t in range(4):
        await_on(m1.at[pl.ds(4 * t, 4)], m1r.at[t])
    mine = mp.at[:, pl.ds(pl.multiple_of(fsd * 16, 16), 16), :]
    own_map = pltpu.make_async_copy(m1, mine, loc.at[18])
    own_map.start()
    for d in range(1, 8):
        rdma(m1, mine, m2s.at[d - 1], m2r.at[d - 1], (ctx, (fsd + d) % 8)).start()

    for n in range(2):
        dst = (kh, vh)[n]
        for d in range(1, 4):
            await_on(dst.at[pl.ds(0, 128), :], kvr.at[n, d - 1])
        await_on(dst.at[pl.ds(0, 128), :], loc.at[n])
    ones = jnp.where(lax.broadcasted_iota(jnp.int32, (16, BLK), 0) == 0, 1.0, 0.0).astype(BF)
    for n in range(2):
        vt[n, 0:HD, :] = jnp.transpose(vh[:, n * HD : (n + 1) * HD])
        vt[n, HD:EXL, :] = ones
    dvt[...] = jnp.zeros_like(dvt)
    dk[...] = jnp.zeros_like(dk)

    own_map.wait()
    for d in range(1, 8):
        await_on(m1, m2r.at[d - 1])

    def r_dev(i):
        return ((i % 4) * 4 + y, 2 * x + i // 4)

    def to_owner(i, src, dst, ssem, rsem):
        dev = r_dev(i)
        put(src.at[pl.ds(2 * i, 2)], dst.at[r], ssem.at[i], rsem.at[r], dev[0], dev[1])

    def keys_step(i, carry):
        n = i // 4
        cols = pl.ds(pl.multiple_of(n * HD, HD), HD)
        for u in range(2):
            h = 2 * i + u
            mine_t = jnp.transpose(mp[h])
            mt[h] = mine_t
            pos, neg = soft_pair(mm(mine_t[FH:], kh[:, cols], 1, 1))
            both = jnp.concatenate((pos, neg), axis=0)
            kp[h] = both
            feat = both.astype(BF)
            kft[h] = feat
            feat_rows = jnp.transpose(feat)
            kf[h] = feat_rows
            sext[h] = mm(vt[n], feat_rows)[:EXT]
        to_owner(i, sext, rin, ss, sr)
        return carry

    lax.fori_loop(0, 8, keys_step, 0)

    def scan(parts, psem, tot, xsem_s, xsem_r, outs, back, bsem_s, bsem_r, forward):
        for j in range(8):
            await_on(parts.at[j], psem.at[j])
        total = parts[0]
        for j in range(1, 8):
            total = total + parts[j]
        tot[x] = total
        for d in range(1, 4):
            rdma(tot.at[x], tot.at[x], xsem_s.at[d - 1], xsem_r.at[d - 1], (ctx, 2 * ((x + d) % 4) + c)).start()
        if forward:
            await_on(pin, pr)
            acc[...] = pin[...]
        else:
            acc[...] = jnp.zeros_like(acc)
        for d in range(1, 4):
            await_on(tot.at[0], xsem_r.at[d - 1])
        for j in range(4):

            @pl.when((j < x) if forward else (j > x))
            def _():
                acc[...] += tot[j]

        run = acc[...]
        for j in range(8) if forward else reversed(range(8)):
            for u in range(2):
                outs[j, u] = low_ext(run[u])
            run = run + parts[j]
            dev = r_dev(j)
            put(outs.at[j], back.at[pl.ds(2 * r, 2)], bsem_s.at[j], bsem_r.at[r], dev[0], dev[1])

    scan(rin, sr, xin, xs, xr, rout, stl, bs, br, True)

    ahead = lax.broadcasted_iota(jnp.int32, (BLK, BLK), 0) <= lax.broadcasted_iota(jnp.int32, (BLK, BLK), 1)

    def back_copy(i, d):
        t = (y + d) % 4
        return rdma(
            gq.at[pl.ds(pl.multiple_of(t * 128, 128), 128), pl.ds(pl.multiple_of(i * 256, 256), 256)],
            oq.at[:, pl.ds(pl.multiple_of(y * 2048 + i * 256, 256), 256)],
            oqs.at[i, d - 1], oqr.at[i, d - 1], y_dev(t),
        )

    def back_own(i):
        return pltpu.make_async_copy(
            gq.at[own_rows, pl.ds(pl.multiple_of(i * 256, 256), 256)],
            oq.at[:, pl.ds(pl.multiple_of(y * 2048 + i * 256, 256), 256)],
            loc.at[19 + i],
        )

    def queries_step(i, carry):
        n = i // 4
        await_on(stl.at[pl.ds(2 * i, 2)], br.at[i])
        for s in range(2):
            for d in range(1, 4):
                qg_copy(i, s, d).wait_recv()
            qg_own(i, s).wait()
        vcols = pl.ds(pl.multiple_of(n * HD, HD), HD)
        for u in range(2):
            h = 2 * i + u
            cols = pl.ds(pl.multiple_of(h * HD, HD), HD)
            qv = qh[:, cols]
            mq = mt[h, 0:FH]
            pos, neg = soft_pair(mm(mq, qv, 1, 1))
            qft = jnp.concatenate((pos, neg), axis=0).astype(BF)
            st = jnp.where(ahead, mm(kf[h], qft), 0.0)
            stlow = st.astype(BF)
            ext = stl[h]
            inter = mm(ext, qft)
            num = inter[:HD] + mm(vt[n, 0:HD], stlow)
            den = (inter[HD : HD + 1] + inter[HD + 1 : HD + 2] + inter[HD + 2 : HD + 3]) + jnp.sum(
                st, axis=0, keepdims=True
            )
            inv = 1.0 / den
            sc = jnp.transpose(gh[:, cols]).astype(F32) * inv
            scl = sc.astype(BF)
            ng = -jnp.sum(sc * (num * inv), axis=0, keepdims=True)
            dst = jnp.where(ahead, mm(vh[:, vcols], scl) + ng, 0.0).astype(BF)
            dfq = mm(ext[:HD], scl, 0, 0) + norm_column(ext) * ng + mm(kft[h], dst)
            dfk[h] = mm(qft, dst, 1, 1)
            dvt[n] += mm(scl, stlow, 1, 1)
            part = mm(jnp.concatenate((scl, three_rows(ng, 16)), axis=0), qft, 1, 1)
            uext[h, 0:HD] = part[:HD]
            row = part[HD : HD + 1] + part[HD + 1 : HD + 2] + part[HD + 2 : HD + 3]
            at = lax.broadcasted_iota(jnp.int32, (8, HD), 0)
            uext[h, HD:EXT] = jnp.where(at == 0, jnp.broadcast_to(row, (8, HD)), 0.0)
            dlt = soft_back(pos, neg, dfq)
            gq[:, cols] = mm(jnp.transpose(dlt), mq).astype(BF)
            gmt[h, 0:FH] = mm(dlt, qv)
        to_owner(i, uext, uin, us, ur)
        for d in range(1, 4):
            back_copy(i, d).start()
        back_own(i).start()
        return carry

    lax.fori_loop(0, 8, queries_step, 0)

    scan(uin, ur, yin, ys, yr, uout, sul, cs, cr, False)

    whole = yin[0] + yin[1] + yin[2] + yin[3]
    for u in range(2):
        pgs[u] = jnp.transpose(whole[u, :HD])
    own_ctx = y * 4 + r // 2
    half = pl.ds(2 * (r % 2), 2)
    for e in range(2):
        put(
            pgs.at[:, pl.ds(pl.multiple_of((2 * x + e) * 16, 16), 16), :], op.at[half],
            gs.at[e], gr.at[r % 2], own_ctx, 2 * x + e,
        )

    def kv_copy(n, s, d):
        src, dst = ((gk, ok), (gv, ov))[s]
        t = (y + d) % 4
        cols = pl.ds(pl.multiple_of(n * HD, HD), HD)
        return rdma(
            src.at[pl.ds(pl.multiple_of(t * 128, 128), 128), cols],
            dst.at[:, pl.ds(pl.multiple_of(y * 256 + n * HD, HD), HD)],
            kos.at[n, s, d - 1], kor.at[n, s, d - 1], y_dev(t),
        )

    def kv_own(n, s):
        src, dst = ((gk, ok), (gv, ov))[s]
        cols = pl.ds(pl.multiple_of(n * HD, HD), HD)
        return pltpu.make_async_copy(
            src.at[own_rows, cols], dst.at[:, pl.ds(pl.multiple_of(y * 256 + n * HD, HD), HD)],
            loc.at[27 + 2 * n + s],
        )

    def finish_step(i, carry):
        n = i // 4
        cols = pl.ds(pl.multiple_of(n * HD, HD), HD)
        await_on(sul.at[pl.ds(2 * i, 2)], cr.at[i])
        for u in range(2):
            h = 2 * i + u
            suf = sul[h]
            up = dfk[h] + mm(suf[:HD], vt[n, 0:HD], 0, 0) + norm_column(suf)
            dvt[n] += mm(suf[:HD], kft[h])
            both = kp[h]
            dlt = soft_back(both[:FH], both[FH:], up)
            dk[n] += mm(jnp.transpose(dlt), mt[h, FH:HD])
            gmt[h, FH:HD] = mm(dlt, kh[:, cols])
            gm[h] = jnp.transpose(gmt[h]).astype(BF)
        to_owner(i, gm, rm, ms, mr)

        @pl.when(i % 4 == 3)
        def _():
            gk[:, cols] = dk[n].astype(BF)
            gv[:, cols] = jnp.transpose(dvt[n]).astype(BF)
            for s in range(2):
                for d in range(1, 4):
                    kv_copy(n, s, d).start()
                kv_own(n, s).start()

        return carry

    lax.fori_loop(0, 8, finish_step, 0)

    for j in range(8):
        await_on(rm.at[j], mr.at[j])
    total = rm[0].astype(F32)
    for j in range(1, 8):
        total = total + rm[j].astype(F32)
    low = total.astype(BF)
    for j in range(4):
        xms[j] = low[:, 32 * j : 32 * (j + 1), :]
    for d in range(1, 4):
        t = (x + d) % 4
        rdma(xms.at[t], xm.at[x], ns.at[d - 1], nr.at[d - 1], (ctx, 2 * t + c)).start()
    xm[x] = xms[x]
    for d in range(1, 4):
        await_on(xm.at[0], nr.at[d - 1])
    summed = xm[0].astype(F32) + xm[1].astype(F32) + xm[2].astype(F32) + xm[3].astype(F32)
    for e in range(2):
        fms[e] = summed[:, 16 * e : 16 * (e + 1), :]
    for e in range(2):
        put(fms.at[e], om.at[half], fs.at[e], fr.at[r % 2], own_ctx, 2 * x + e)

    for e in range(2):
        await_on(fms.at[e], fr.at[e])
        await_on(fms.at[e], gr.at[e])
        sent(fms.at[e], fs.at[e], own_ctx, 2 * x + e)
        sent(fms.at[e], gs.at[e], own_ctx, 2 * x + e)
    for d in range(3):
        await_on(xm.at[0], ns.at[d])
        await_on(xin.at[0], xs.at[d])
        await_on(yin.at[0], ys.at[d])
    for t in range(4):
        sent(maps, m1s.at[t], t * 4 + z, fsd)
    sent(pin, ps, pre_ctx, pre_f)
    for d in range(7):
        await_on(m1, m2s.at[d])
    for n in range(2):
        for d in range(1, 4):
            await_on(kh.at[pl.ds(0, 128), :], kvs.at[n, d - 1])
        for s in range(2):
            for d in range(1, 4):
                kv_copy(n, s, d).wait()
            kv_own(n, s).wait()

    def drain(i, carry):
        for s in range(2):
            for d in range(1, 4):
                qg_copy(i, s, d).wait_send()
        for d in range(1, 4):
            back_copy(i, d).wait()
        back_own(i).wait()
        dev = r_dev(i)
        sent(rin.at[0], ss.at[i], dev[0], dev[1])
        sent(rin.at[0], us.at[i], dev[0], dev[1])
        sent(rm.at[0], ms.at[i], dev[0], dev[1])
        sent(rout.at[0], bs.at[i], dev[0], dev[1])
        sent(rout.at[0], cs.at[i], dev[0], dev[1])
        return carry

    lax.fori_loop(0, 8, drain, 0)


def shards(query_rows, key_rows, value_rows, grad_out, query_map, key_map, prefix_state, prefix_norm):
    maps = jnp.concatenate((query_map, key_map), axis=-1)
    pext = jnp.concatenate(
        (
            jnp.swapaxes(prefix_state, 1, 2),
            prefix_norm[:, None, :],
            jnp.zeros((4, EXT - HD - 1, HD), F32),
        ),
        axis=1,
    )
    dma = lambda *s: pltpu.SemaphoreType.DMA(s)
    vm = lambda dt, *s: pltpu.VMEM(s, dt)
    outs = pl.pallas_call(
        kernel,
        out_shape=(
            jax.ShapeDtypeStruct((128, 8192), BF),
            jax.ShapeDtypeStruct((128, 1024), BF),
            jax.ShapeDtypeStruct((128, 1024), BF),
            jax.ShapeDtypeStruct((4, 16, 128), F32),
            jax.ShapeDtypeStruct((4, 16, 128), F32),
        ),
        in_specs=[pl.BlockSpec(memory_space=pl.ANY)] * 6,
        out_specs=[pl.BlockSpec(memory_space=pl.ANY)] * 5,
        scratch_shapes=[
            vm(BF, 16, 16, 128), vm(BF, 16, 128, 128), vm(BF, 16, 128, 128),
            vm(BF, 512, 2048), vm(BF, 512, 2048), vm(BF, 512, 256), vm(BF, 512, 256),
            vm(BF, 2, EXL, 512), vm(BF, 16, 512, 128), vm(BF, 16, 128, 512), vm(F32, 16, 128, 512),
            vm(F32, 16, EXT, 128), vm(F32, 16, EXT, 128),
            vm(F32, 8, 2, EXT, 128), vm(F32, 8, 2, EXT, 128),
            vm(F32, 4, 2, EXT, 128), vm(F32, 4, 2, EXT, 128), vm(F32, 2, EXT, 128),
            vm(BF, 8, 2, EXL, 128), vm(BF, 8, 2, EXL, 128),
            vm(BF, 16, EXL, 128), vm(BF, 16, EXL, 128),
            vm(F32, 16, 128, 512), vm(F32, 2, 128, 512), vm(F32, 2, 512, 128),
            vm(BF, 512, 2048), vm(F32, 16, 128, 128), vm(BF, 16, 128, 128), vm(BF, 8, 2, 128, 128),
            vm(BF, 4, 2, 32, 128), vm(BF, 4, 2, 32, 128), vm(F32, 2, 2, 16, 128), vm(F32, 2, 128, 128),
            vm(BF, 512, 256), vm(BF, 512, 256), vm(F32, 2, EXT, 128),
            dma(4), dma(4), dma(7), dma(7), dma(), dma(), dma(2, 3), dma(2, 3),
            dma(8, 2, 3), dma(8, 2, 3), dma(31),
            dma(8), dma(8), dma(3), dma(3), dma(8), dma(8),
            dma(8), dma(8), dma(3), dma(3), dma(8), dma(8),
            dma(8, 3), dma(8, 3), dma(2, 2, 3), dma(2, 2, 3),
            dma(8), dma(8), dma(3), dma(3), dma(2), dma(2), dma(2), dma(2),
        ],
        compiler_params=pltpu.CompilerParams(
            collective_id=0, has_side_effects=True, vmem_limit_bytes=60 * 1024 * 1024
        ),
    )(maps, pext, query_rows, grad_out, key_rows, value_rows)
    grad_q, grad_k, grad_v, grad_m, grad_p = outs
    return (grad_q, grad_k, grad_v, grad_m[..., :FH], grad_m[..., FH:], grad_p)


def solution(mesh):
    both = ("fsdp", "ctx")
    rows = P(both, None)
    return jax.shard_map(
        shards,
        mesh=mesh,
        in_specs=(
            rows, rows, rows, rows,
            P("ctx", "fsdp", None), P("ctx", "fsdp", None),
            P("ctx", None, None), P("ctx", None),
        ),
        out_specs=(
            rows, rows, rows,
            P("ctx", "fsdp", None), P("ctx", "fsdp", None), P("ctx", "fsdp", None),
        ),
        check_vma=False,
    )
```

```python
import functools

import jax
import jax.numpy as jnp
from jax import lax
from jax.experimental import pallas as pl
from jax.experimental.pallas import tpu as pltpu
from jax.sharding import PartitionSpec as P

HD = 128
FH = 64
BLK = 512
EXT = 136
EXL = 144
LAG = 5
SHARE = 3
OUT = 9
BACK = 11
MESH = pl.DeviceIdType.MESH
F32 = jnp.float32
BF = jnp.bfloat16


def mm(a, b, ca=1, cb=0):
    return lax.dot_general(a, b, (((ca,), (cb,)), ((), ())), preferred_element_type=F32)


def soft_pair(logits):
    wide = logits.astype(BF).astype(F32)
    up = jnp.exp(wide)
    low = jnp.exp(-wide)
    pos = up * (1.0 / jnp.sum(up, axis=0, keepdims=True))
    neg = low * (1.0 / jnp.sum(low, axis=0, keepdims=True))
    return pos, neg


def soft_back(pos, neg, up):
    one = up[:FH]
    two = up[FH:]
    first = pos * (one - jnp.sum(pos * one, axis=0, keepdims=True))
    second = neg * (two - jnp.sum(neg * two, axis=0, keepdims=True))
    return (first - second).astype(BF)


def three_rows(row, height):
    high = row.astype(BF).astype(F32)
    rest = row - high
    mid = rest.astype(BF).astype(F32)
    last = rest - mid
    at = lax.broadcasted_iota(jnp.int32, (height, row.shape[1]), 0)
    zero = jnp.zeros((height, row.shape[1]), F32)
    out = jnp.where(at == 0, high, jnp.where(at == 1, mid, jnp.where(at == 2, last, zero)))
    return out.astype(BF)


def low_ext(wide):
    return jnp.concatenate((wide[:HD].astype(BF), three_rows(wide[HD : HD + 1], 16)), axis=0)


def wide_ext(low):
    tail = low[HD:EXL].astype(F32)
    row = tail[0:1] + tail[1:2] + tail[2:3]
    return jnp.concatenate((low[:HD].astype(F32), jnp.broadcast_to(row, (8, HD))), axis=0)


def norm_column(low):
    tail = low[HD:EXL].astype(F32)
    row = tail[0:1] + tail[1:2] + tail[2:3]
    return jnp.transpose(jnp.broadcast_to(row, (8, HD)))[:, 0:1]


def kernel(
    qmap, kmap, pst, pnm, q, g, k, v,
    odl, omq, ok, ov, om, op,
    qin, kin, nin, maps, nblk, m1, mq2, mp, mt, qgh, kvh, vt, kf, kft, kp,
    sext, uext, rin, uin, xin, yin, praw, pnr, rout, uout, stl, sul,
    dfk, dvt, dk, qp, qf, sts, scs, ngs, dl, gmt, gm, rm, low, fmr, fmo, pgs, gkv, acc,
    m1s, m1r, m2s, m2r, m3s, m3r, ps, pr, kvs, kvr, qgs, qgr, loc,
    ss, sr, xs, xr, bs, br, us, ur, ys, yr, cs, cr, oqs, oqr, kos, kor,
    ms, mr, fs, fr, gs, gr,
):
    ctx = lax.axis_index("ctx")
    fsd = lax.axis_index("fsdp")
    z = ctx // 4
    y = ctx % 4
    x = fsd // 2
    c = fsd % 2
    r = c * 4 + z

    def rdma(src, dst, ssem, rsem, dev):
        return pltpu.make_async_remote_copy(
            src_ref=src, dst_ref=dst, send_sem=ssem, recv_sem=rsem, device_id=dev, device_id_type=MESH
        )

    def await_on(ref, sem):
        pltpu.make_async_copy(ref, ref, sem).wait()

    first = [
        pltpu.make_async_copy(qmap, qin, loc.at[0]),
        pltpu.make_async_copy(kmap, kin, loc.at[1]),
        pltpu.make_async_copy(pnm, nin, loc.at[2]),
    ]
    for copy in first:
        copy.start()
    other = fsd + 1 - 2 * c
    barrier = pltpu.get_barrier_semaphore()
    for j in range(1, 8):
        pl.semaphore_signal(barrier, inc=1, device_id=(ctx, (fsd + j) % 8), device_id_type=MESH)

    def greet(j, carry):
        at = (ctx + j) % 16
        for e in range(4):
            pl.semaphore_signal(barrier, inc=1, device_id=(at, 2 * e + c), device_id_type=MESH)
            pl.semaphore_signal(barrier, inc=1, device_id=(at, 2 * e + 1 - c), device_id_type=MESH)
        return carry

    lax.fori_loop(1, 16, greet, 0)
    for copy in first:
        copy.wait()
    maps[...] = jnp.concatenate((qin[...], kin[...]), axis=-1)
    norms = jnp.where(c == 0, nin[0:2, :], nin[2:4, :])
    for u in range(2):
        nblk[u] = jnp.broadcast_to(norms[u : u + 1], (8, HD))
    pl.semaphore_wait(barrier, 127)

    def y_dev(t):
        return (z * 4 + t, fsd)

    own_rows = pl.ds(y * 128, 128)

    def put(src, dst, ssem, rsem, dev_ctx, dev_f):
        is_me = jnp.logical_and(dev_ctx == ctx, dev_f == fsd)

        @pl.when(is_me)
        def _():
            pltpu.make_async_copy(src, dst, rsem).start()

        @pl.when(jnp.logical_not(is_me))
        def _():
            rdma(src, dst, ssem, rsem, (dev_ctx, dev_f)).start()

    def sent(src, ssem, dev_ctx, dev_f):
        is_me = jnp.logical_and(dev_ctx == ctx, dev_f == fsd)

        @pl.when(jnp.logical_not(is_me))
        def _():
            await_on(src, ssem)

    def map_to(dev_ctx, urgent):
        put(maps, m1.at[pl.ds(4 * ctx, 4)], m1s, m1r.at[urgent], dev_ctx, fsd)

    for t in range(4):
        map_to(t * 4 + z, 0)
    pre_ctx = (2 * (y % 2) + c) * 4 + z
    pre_f = 2 * x + y // 2

    for n, src in enumerate((k, v)):
        dst = kvh.at[n, own_rows, :]
        for d in range(1, 4):
            t = (y + d) % 4
            rdma(src.at[:, pl.ds(pl.multiple_of(t * 256, 256), 256)], dst, kvs, kvr, y_dev(t)).start()
        pltpu.make_async_copy(src.at[:, pl.ds(pl.multiple_of(y * 256, 256), 256)], dst, kvr).start()

    def qg_start(i, carry):
        cols = pl.ds(pl.multiple_of(i * 256, 256), 256)
        for n, src in enumerate((q, g)):
            dst = qgh.at[n, own_rows, cols]
            for d in range(1, 4):
                t = (y + d) % 4
                part = src.at[:, pl.ds(pl.multiple_of(t * 2048 + i * 256, 256), 256)]
                rdma(part, dst, qgs, qgr.at[i], y_dev(t)).start()
            part = src.at[:, pl.ds(pl.multiple_of(y * 2048 + i * 256, 256), 256)]
            pltpu.make_async_copy(part, dst, qgr.at[i]).start()
        return carry

    lax.fori_loop(0, 1, qg_start, 0)
    await_on(m1.at[pl.ds(0, 16)], m1r.at[0])
    own_heads = m1.at[pl.ds(16 * y, 16)]
    mine = mp.at[:, pl.ds(pl.multiple_of(fsd * 16, 16), 16), :]
    pltpu.make_async_copy(own_heads, mine, m2r).start()
    for d in range(1, 8):
        rdma(own_heads, mine, m2s, m2r, (ctx, (fsd + d) % 8)).start()
    put(pst.at[pl.ds(2 * c, 2)], praw, ps.at[0], pr.at[0], pre_ctx, pre_f)
    put(nblk, pnr, ps.at[1], pr.at[1], pre_ctx, pre_f)
    for d in range(1, 4):
        for t in range(4):
            map_to(t * 4 + (z + d) % 4, 1)
    lax.fori_loop(1, 8, qg_start, 0)

    await_on(kvh, kvr)
    ones = jnp.where(lax.broadcasted_iota(jnp.int32, (16, BLK), 0) == 0, 1.0, 0.0).astype(BF)
    for n in range(2):
        vt[n, 0:HD, :] = jnp.transpose(kvh[1, :, n * HD : (n + 1) * HD])
        vt[n, HD:EXL, :] = ones
    dvt[...] = jnp.zeros_like(dvt)
    dk[...] = jnp.zeros_like(dk)

    await_on(mp, m2r)

    def r_dev(i):
        return ((i % 4) * 4 + y, 2 * x + i // 4)

    def to_owner(i, src, dst, ssem, rsem):
        dev = r_dev(i)
        put(src.at[pl.ds(2 * i, 2)], dst.at[r], ssem, rsem, dev[0], dev[1])

    def keys_step(i, carry):
        n = i // 4
        cols = pl.ds(pl.multiple_of(n * HD, HD), HD)
        for u in range(2):
            h = 2 * i + u
            mine_t = jnp.transpose(mp[h])
            mt[h] = mine_t
            pos, neg = soft_pair(mm(mine_t[FH:], kvh[0, :, cols], 1, 1))
            both = jnp.concatenate((pos, neg), axis=0)
            kp[h] = both
            feat = both.astype(BF)
            kft[h] = feat
            feat_rows = jnp.transpose(feat)
            kf[h] = feat_rows
            sext[h] = low_ext(mm(vt[n], feat_rows))
        to_owner(i, sext, rin, ss, sr)
        return carry

    lax.fori_loop(0, 8, keys_step, 0)

    def scan_out(parts, psem, tot, xsem_s, xsem_r):
        await_on(parts, psem)
        for u in range(2):
            total = wide_ext(parts[0, u])
            for j in range(1, 8):
                total = total + wide_ext(parts[j, u])
            tot[x, u] = low_ext(total)
        for d in range(1, 4):
            rdma(tot.at[x], tot.at[x], xsem_s, xsem_r, (ctx, 2 * ((x + d) % 4) + c)).start()

    def scan_back(parts, tot, xsem_r, outs, back, bsem_s, bsem_r, forward):
        if forward:
            await_on(praw, pr.at[0])
            await_on(pnr, pr.at[1])
            for u in range(2):
                acc[u, 0:HD] = jnp.transpose(praw[u])
                acc[u, HD:EXT] = pnr[u]
        else:
            acc[...] = jnp.zeros_like(acc)
        await_on(tot.at[pl.ds(0, 3)], xsem_r)
        for j in range(4):

            @pl.when((j < x) if forward else (j > x))
            def _():
                for u in range(2):
                    acc[u] += wide_ext(tot[j, u])

        run = [acc[0], acc[1]]
        for j in range(8) if forward else reversed(range(8)):
            for u in range(2):
                outs[j, u] = low_ext(run[u])
                run[u] = run[u] + wide_ext(parts[j, u])
            dev = r_dev(j)
            put(outs.at[j], back.at[pl.ds(2 * r, 2)], bsem_s, bsem_r.at[r], dev[0], dev[1])

    scan_out(rin, sr, xin, xs, xr)
    scan_back(rin, xin, xr, rout, stl, bs, br, True)
    part_q = omq.at[:, pl.ds(pl.multiple_of(fsd * 16, 16), 16), :]

    def share_maps():
        await_on(m1.at[pl.ds(0, 48)], m1r.at[1])
        for t in range(32):
            mq2[t] = jnp.concatenate((m1[2 * t][:, :FH], m1[2 * t + 1][:, :FH]), axis=-1)
        pltpu.make_async_copy(mq2, part_q, m3r).start()
        for d in range(1, 8):
            rdma(mq2, part_q, m3s, m3r, (ctx, (fsd + d) % 8)).start()

    ahead = lax.broadcasted_iota(jnp.int32, (BLK, BLK), 0) <= lax.broadcasted_iota(jnp.int32, (BLK, BLK), 1)

    def back_start(i):
        lanes = pl.ds(pl.multiple_of(i * 128, 128), 128)
        dst = odl.at[:, pl.ds(pl.multiple_of(y * 1024 + i * 128, 128), 128)]
        for d in range(1, 4):
            t = (y + d) % 4
            rdma(dl.at[pl.ds(pl.multiple_of(t * 128, 128), 128), lanes], dst, oqs, oqr, y_dev(t)).start()
        pltpu.make_async_copy(dl.at[own_rows, lanes], dst, oqr).start()

    def queries_first(i):
        n = i // 4
        await_on(stl.at[pl.ds(2 * i, 2)], br.at[i])
        await_on(qgh.at[:, :, pl.ds(pl.multiple_of(i * 256, 256), 256)], qgr.at[i])
        for u in range(2):
            h = 2 * i + u
            cols = pl.ds(pl.multiple_of(h * HD, HD), HD)
            pos, neg = soft_pair(mm(mt[h, 0:FH], qgh[0, :, cols], 1, 1))
            both = jnp.concatenate((pos, neg), axis=0)
            qp[h] = both
            qft = both.astype(BF)
            qf[h] = qft
            st = jnp.where(ahead, mm(kf[h], qft), 0.0)
            stlow = st.astype(BF)
            sts[h] = stlow
            inter = mm(stl[h], qft)
            num = inter[:HD] + mm(vt[n, 0:HD], stlow)
            den = (inter[HD : HD + 1] + inter[HD + 1 : HD + 2] + inter[HD + 2 : HD + 3]) + jnp.sum(
                st, axis=0, keepdims=True
            )
            inv = 1.0 / den
            sc = jnp.transpose(qgh[1, :, cols]).astype(F32) * inv
            scl = sc.astype(BF)
            scs[h] = scl
            ng = -jnp.sum(sc * (num * inv), axis=0, keepdims=True)
            ngs[h] = ng
            part = mm(jnp.concatenate((scl, three_rows(ng, 16)), axis=0), qft, 1, 1)
            row = part[HD : HD + 1] + part[HD + 1 : HD + 2] + part[HD + 2 : HD + 3]
            uext[h] = jnp.concatenate((part[:HD].astype(BF), three_rows(row, 16)), axis=0)
        to_owner(i, uext, uin, us, ur)

    def queries_second(i):
        n = i // 4
        vcols = pl.ds(pl.multiple_of(n * HD, HD), HD)
        logs = []
        for u in range(2):
            h = 2 * i + u
            cols = pl.ds(pl.multiple_of(h * HD, HD), HD)
            scl = scs[h]
            ng = ngs[h]
            qft = qf[h]
            ext = stl[h]
            dst = jnp.where(ahead, mm(kvh[1, :, vcols], scl) + ng, 0.0).astype(BF)
            dfq = mm(ext[:HD], scl, 0, 0) + norm_column(ext) * ng + mm(kft[h], dst)
            dfk[h] = mm(qft, dst, 1, 1)
            dvt[n] += mm(scl, sts[h], 1, 1)
            both = qp[h]
            dlt = soft_back(both[:FH], both[FH:], dfq)
            logs.append(dlt)
            gmt[h, 0:FH] = mm(dlt, qgh[0, :, cols])
        dl[:, pl.ds(pl.multiple_of(i * 128, 128), 128)] = jnp.transpose(jnp.concatenate(logs, axis=0))
        back_start(i)

    def queries_step(t, carry):
        @pl.when(t < 8)
        def _():
            queries_first(t)

        @pl.when(t >= LAG)
        def _():
            queries_second(t - LAG)

        @pl.when(t == SHARE)
        def _():
            share_maps()

        @pl.when(t == OUT)
        def _():
            scan_out(uin, ur, yin, ys, yr)

        @pl.when(t == BACK)
        def _():
            scan_back(uin, yin, yr, uout, sul, cs, cr, False)

        return carry

    lax.fori_loop(0, 8 + LAG, queries_step, 0)

    for u in range(2):
        whole = yin[0, u, :HD].astype(F32)
        for j in range(1, 4):
            whole = whole + yin[j, u, :HD].astype(F32)
        pgs[u] = jnp.transpose(whole)
    own_ctx = y * 4 + r // 2
    half = pl.ds(2 * (r % 2), 2)
    for e in range(2):
        put(
            pgs.at[:, pl.ds(pl.multiple_of((2 * x + e) * 16, 16), 16), :], op.at[half],
            gs, gr, own_ctx, 2 * x + e,
        )

    def kv_start(n):
        cols = pl.ds(pl.multiple_of(n * HD, HD), HD)
        for s, out in enumerate((ok, ov)):
            dst = out.at[:, pl.ds(pl.multiple_of(y * 256 + n * HD, HD), HD)]
            for d in range(1, 4):
                t = (y + d) % 4
                part = gkv.at[s, pl.ds(pl.multiple_of(t * 128, 128), 128), cols]
                rdma(part, dst, kos, kor.at[s], y_dev(t)).start()
            pltpu.make_async_copy(gkv.at[s, own_rows, cols], dst, kor.at[s]).start()

    def finish_step(i, carry):
        n = i // 4
        cols = pl.ds(pl.multiple_of(n * HD, HD), HD)
        await_on(sul.at[pl.ds(2 * i, 2)], cr.at[i])
        for u in range(2):
            h = 2 * i + u
            suf = sul[h]
            up = dfk[h] + mm(suf[:HD], vt[n, 0:HD], 0, 0) + norm_column(suf)
            dvt[n] += mm(suf[:HD], kft[h])
            both = kp[h]
            dlt = soft_back(both[:FH], both[FH:], up)
            dk[n] += mm(jnp.transpose(dlt), mt[h, FH:HD])
            gmt[h, FH:HD] = mm(dlt, kvh[0, :, cols])
            gm[h] = jnp.transpose(gmt[h]).astype(BF)
        to_owner(i, gm, rm, ms, mr)

        @pl.when(i % 4 == 3)
        def _():
            gkv[0, :, cols] = dk[n].astype(BF)
            gkv[1, :, cols] = jnp.transpose(dvt[n]).astype(BF)
            kv_start(n)

        return carry

    lax.fori_loop(0, 8, finish_step, 0)

    await_on(rm, mr)
    total = rm[0].astype(F32)
    for j in range(1, 8):
        total = total + rm[j].astype(F32)
    low[...] = total.astype(BF)
    for e in range(8):
        to = (fsd + e) % 8
        put(
            low.at[:, pl.ds(pl.multiple_of(to * 16, 16), 16), :], fmr.at[x, half],
            fs, fr, own_ctx, to,
        )
    await_on(fmr, fr)
    fmo[...] = (fmr[0].astype(F32) + fmr[1].astype(F32)) + (fmr[2].astype(F32) + fmr[3].astype(F32))
    last = pltpu.make_async_copy(fmo, om, loc.at[0])
    last.start()

    await_on(op, gr)
    here = own_ctx == ctx

    @pl.when(here)
    def _():
        await_on(op.at[pl.ds(0, 2)], gs)
        await_on(low.at[:, pl.ds(0, 112), :], fs)

    @pl.when(jnp.logical_not(here))
    def _():
        await_on(op, gs)
        await_on(low, fs)

    await_on(xin.at[pl.ds(0, 3)], xs)
    await_on(yin.at[pl.ds(0, 3)], ys)
    await_on(m1.at[pl.ds(0, 60)], m1s)
    sent(praw, ps.at[0], pre_ctx, pre_f)
    sent(pnr, ps.at[1], pre_ctx, pre_f)
    await_on(mp.at[:, pl.ds(0, 112), :], m2s)
    await_on(omq.at[:, pl.ds(0, 112), :], m3s)
    await_on(omq, m3r)
    await_on(kvh.at[:, pl.ds(0, 384), :], kvs)
    await_on(qgh.at[:, pl.ds(0, 384), :], qgs)
    await_on(dl.at[pl.ds(0, 384), :], oqs)
    await_on(odl, oqr)
    await_on(gkv.at[:, pl.ds(0, 384), :], kos)
    await_on(ok, kor.at[0])
    await_on(ov, kor.at[1])
    for sem in (ss, us):
        await_on(rin.at[pl.ds(0, 7)], sem)
    for sem in (bs, cs):
        await_on(rout.at[pl.ds(0, 7)], sem)
    await_on(rm.at[pl.ds(0, 7)], ms)
    last.wait()


def close(dl, mq, k, v, m, p, oq, ok, ov, omq, omk, op):
    i = pl.program_id(0)
    lane = lax.broadcasted_iota(jnp.int32, (HD, HD), 1)
    for t in range(8):
        pair = mq[t]
        zero = jnp.zeros_like(pair)
        wide = jnp.concatenate((jnp.where(lane < FH, pair, zero), jnp.where(lane < FH, zero, pair)), axis=0)
        oq[:, 2 * t * HD : 2 * (t + 1) * HD] = mm(dl[:, t * HD : (t + 1) * HD], wide, 1, 1).astype(BF)

    ok[...] = k[...]
    ov[...] = v[...]

    @pl.when(i == 0)
    def _():
        omq[...] = m[:, :, :FH]
        omk[...] = m[:, :, FH:]
        op[...] = p[...]


def shards(query_rows, key_rows, value_rows, grad_out, query_map, key_map, prefix_state, prefix_norm):
    dma = lambda *s: pltpu.SemaphoreType.DMA(s)
    vm = lambda dt, *s: pltpu.VMEM(s, dt)
    outs = pl.pallas_call(
        kernel,
        out_shape=(
            jax.ShapeDtypeStruct((128, 4096), BF),
            jax.ShapeDtypeStruct((32, 128, 128), BF),
            jax.ShapeDtypeStruct((128, 1024), BF),
            jax.ShapeDtypeStruct((128, 1024), BF),
            jax.ShapeDtypeStruct((4, 16, 128), F32),
            jax.ShapeDtypeStruct((4, 16, 128), F32),
        ),
        in_specs=[pl.BlockSpec(memory_space=pl.ANY)] * 8,
        out_specs=[pl.BlockSpec(memory_space=pl.ANY)] * 6,
        scratch_shapes=[
            vm(BF, 4, 16, 64), vm(BF, 4, 16, 64), vm(F32, 4, 128), vm(BF, 4, 16, 128), vm(F32, 2, 8, 128),
            vm(BF, 64, 16, 128), vm(BF, 32, 16, 128), vm(BF, 16, 128, 128), vm(BF, 16, 128, 128),
            vm(BF, 2, 512, 2048), vm(BF, 2, 512, 256),
            vm(BF, 2, EXL, 512), vm(BF, 16, 512, 128), vm(BF, 16, 128, 512), vm(F32, 16, 128, 512),
            vm(BF, 16, EXL, 128), vm(BF, 16, EXL, 128),
            vm(BF, 8, 2, EXL, 128), vm(BF, 8, 2, EXL, 128),
            vm(BF, 4, 2, EXL, 128), vm(BF, 4, 2, EXL, 128), vm(F32, 2, 128, 128), vm(F32, 2, 8, 128),
            vm(BF, 8, 2, EXL, 128), vm(BF, 8, 2, EXL, 128),
            vm(BF, 16, EXL, 128), vm(BF, 16, EXL, 128),
            vm(F32, 16, 128, 512), vm(F32, 2, 128, 512), vm(F32, 2, 512, 128),
            vm(F32, 16, 128, 512), vm(BF, 16, 128, 512), vm(BF, 16, 512, 512), vm(BF, 16, 128, 512), vm(F32, 16, 1, 512),
            vm(BF, 512, 1024), vm(F32, 16, 128, 128), vm(BF, 16, 128, 128), vm(BF, 8, 2, 128, 128),
            vm(BF, 2, 128, 128), vm(BF, 4, 4, 16, 128), vm(F32, 4, 16, 128), vm(F32, 2, 128, 128),
            vm(BF, 2, 512, 256), vm(F32, 2, EXT, 128),
            dma(), dma(2), dma(), dma(), dma(), dma(), dma(2), dma(2), dma(), dma(), dma(), dma(8), dma(3),
            dma(), dma(), dma(), dma(), dma(), dma(8), dma(), dma(), dma(), dma(), dma(), dma(8), dma(), dma(), dma(), dma(2),
            dma(), dma(), dma(), dma(), dma(), dma(),
        ],
        compiler_params=pltpu.CompilerParams(
            collective_id=0, has_side_effects=True, vmem_limit_bytes=60 * 1024 * 1024
        ),
    )(query_map, key_map, prefix_state, prefix_norm, query_rows, grad_out, key_rows, value_rows)
    log_q, map_q, grad_k, grad_v, grad_m, grad_p = outs
    whole = lambda *s: pl.BlockSpec(s, lambda i: (0,) * len(s))
    return pl.pallas_call(
        close,
        grid=(4,),
        out_shape=(
            jax.ShapeDtypeStruct((128, 8192), BF),
            jax.ShapeDtypeStruct((128, 1024), BF),
            jax.ShapeDtypeStruct((128, 1024), BF),
            jax.ShapeDtypeStruct((4, 16, 64), F32),
            jax.ShapeDtypeStruct((4, 16, 64), F32),
            jax.ShapeDtypeStruct((4, 16, 128), F32),
        ),
        in_specs=[
            pl.BlockSpec((128, 1024), lambda i: (0, i)),
            pl.BlockSpec((8, 128, 128), lambda i: (i, 0, 0)),
            pl.BlockSpec((128, 256), lambda i: (0, i)),
            pl.BlockSpec((128, 256), lambda i: (0, i)),
            whole(4, 16, 128),
            whole(4, 16, 128),
        ],
        out_specs=[
            pl.BlockSpec((128, 2048), lambda i: (0, i)),
            pl.BlockSpec((128, 256), lambda i: (0, i)),
            pl.BlockSpec((128, 256), lambda i: (0, i)),
            whole(4, 16, 64),
            whole(4, 16, 64),
            whole(4, 16, 128),
        ],
    )(log_q, map_q, grad_k, grad_v, grad_m, grad_p)


def solution(mesh):
    both = ("fsdp", "ctx")
    rows = P(both, None)
    return jax.shard_map(
        shards,
        mesh=mesh,
        in_specs=(
            rows, rows, rows, rows,
            P("ctx", "fsdp", None), P("ctx", "fsdp", None),
            P("ctx", None, None), P("ctx", None),
        ),
        out_specs=(
            rows, rows, rows,
            P("ctx", "fsdp", None), P("ctx", "fsdp", None), P("ctx", "fsdp", None),
        ),
        check_vma=False,
    )
```

```python
import functools

import jax
import jax.numpy as jnp
from jax import lax
from jax.experimental import pallas as pl
from jax.experimental.pallas import tpu as pltpu
from jax.sharding import PartitionSpec as P

HD = 128
FH = 64
BLK = 512
EXT = 136
EXL = 144
LAG = 8
OUT = 8
BACK = 11
EARLY = 4
MAP = 4
LATE = 3
MESH = pl.DeviceIdType.MESH
F32 = jnp.float32
BF = jnp.bfloat16


def mm(a, b, ca=1, cb=0):
    return lax.dot_general(a, b, (((ca,), (cb,)), ((), ())), preferred_element_type=F32)


def soft_pair(logits):
    wide = logits.astype(BF).astype(F32)
    up = jnp.exp(wide)
    low = jnp.exp(-wide)
    pos = up * (1.0 / jnp.sum(up, axis=0, keepdims=True))
    neg = low * (1.0 / jnp.sum(low, axis=0, keepdims=True))
    return pos, neg


def soft_back(pos, neg, up):
    one = up[:FH]
    two = up[FH:]
    first = pos * (one - jnp.sum(pos * one, axis=0, keepdims=True))
    second = neg * (two - jnp.sum(neg * two, axis=0, keepdims=True))
    return (first - second).astype(BF)


def three_rows(row, height):
    high = row.astype(BF).astype(F32)
    rest = row - high
    mid = rest.astype(BF).astype(F32)
    last = rest - mid
    at = lax.broadcasted_iota(jnp.int32, (height, row.shape[1]), 0)
    zero = jnp.zeros((height, row.shape[1]), F32)
    out = jnp.where(at == 0, high, jnp.where(at == 1, mid, jnp.where(at == 2, last, zero)))
    return out.astype(BF)


def low_ext(wide):
    return jnp.concatenate((wide[:HD].astype(BF), three_rows(wide[HD : HD + 1], 16)), axis=0)


def wide_ext(low):
    tail = low[HD:EXL].astype(F32)
    row = tail[0:1] + tail[1:2] + tail[2:3]
    return jnp.concatenate((low[:HD].astype(F32), jnp.broadcast_to(row, (8, HD))), axis=0)


def norm_column(low):
    tail = low[HD:EXL].astype(F32)
    row = tail[0:1] + tail[1:2] + tail[2:3]
    return jnp.transpose(jnp.broadcast_to(row, (8, HD)))[:, 0:1]


def kernel(
    qmap, kmap, pst, pnm, q, g, k, v,
    odl, omq, ok, ov, om, op,
    qin, kin, nin, maps, nblk, m1, mk2, mq2, mkp, mqa, mt, qv, lts, lq, gh, kvh, vt, kf, kft, kp,
    sext, uext, rin, uin, xin, yin, praw, pnr, rout, uout, stl, sul,
    dfk, dvt, dk, qp, qf, sts, scs, ngs, dl, dlv, gqs, rq, gks, rk, lowq, lowk, fq, fk, fmo, pgs, gkv, acc,
    m1s, m1r, m2s, m2r, m3s, m3r, ps, pr, kvs, kvr, qgs, qgr, lqs, lqr, loc,
    ss, sr, xs, xr, bs, br, us, ur, ys, yr, cs, cr, oqs, oqr, kos, kor,
    rqs, rqr, rks, rkr, fqs, fqr, fks, fkr, gs, gr,
):
    ctx = lax.axis_index("ctx")
    fsd = lax.axis_index("fsdp")
    z = ctx // 4
    y = ctx % 4
    x = fsd // 2
    c = fsd % 2
    r = c * 4 + z

    def rdma(src, dst, ssem, rsem, dev):
        return pltpu.make_async_remote_copy(
            src_ref=src, dst_ref=dst, send_sem=ssem, recv_sem=rsem, device_id=dev, device_id_type=MESH
        )

    def await_on(ref, sem):
        pltpu.make_async_copy(ref, ref, sem).wait()

    first = [
        pltpu.make_async_copy(qmap, qin, loc.at[0]),
        pltpu.make_async_copy(kmap, kin, loc.at[1]),
        pltpu.make_async_copy(pnm, nin, loc.at[2]),
    ]
    for copy in first:
        copy.start()
    rows_in = pltpu.make_async_copy(q, qv, loc.at[3])
    rows_in.start()
    other = fsd + 1 - 2 * c
    barrier = pltpu.get_barrier_semaphore()
    for j in range(1, 8):
        pl.semaphore_signal(barrier, inc=1, device_id=(ctx, (fsd + j) % 8), device_id_type=MESH)

    def greet(j, carry):
        at = (ctx + j) % 16
        for e in range(4):
            pl.semaphore_signal(barrier, inc=1, device_id=(at, 2 * e + c), device_id_type=MESH)
            pl.semaphore_signal(barrier, inc=1, device_id=(at, 2 * e + 1 - c), device_id_type=MESH)
        return carry

    lax.fori_loop(1, 16, greet, 0)
    for copy in first:
        copy.wait()
    maps[...] = jnp.concatenate((qin[...], kin[...]), axis=-1)
    norms = jnp.where(c == 0, nin[0:2, :], nin[2:4, :])
    for u in range(2):
        nblk[u] = jnp.broadcast_to(norms[u : u + 1], (8, HD))
    pl.semaphore_wait(barrier, 127)

    def y_dev(t):
        return (z * 4 + t, fsd)

    own_rows = pl.ds(y * 128, 128)

    def put(src, dst, ssem, rsem, dev_ctx, dev_f):
        is_me = jnp.logical_and(dev_ctx == ctx, dev_f == fsd)

        @pl.when(is_me)
        def _():
            pltpu.make_async_copy(src, dst, rsem).start()

        @pl.when(jnp.logical_not(is_me))
        def _():
            rdma(src, dst, ssem, rsem, (dev_ctx, dev_f)).start()

    def sent(src, ssem, dev_ctx, dev_f):
        is_me = jnp.logical_and(dev_ctx == ctx, dev_f == fsd)

        @pl.when(jnp.logical_not(is_me))
        def _():
            await_on(src, ssem)

    pltpu.make_async_copy(maps, m1.at[pl.ds(4 * ctx, 4)], m1r).start()
    for j in range(1, 16):
        rdma(maps, m1.at[pl.ds(4 * ctx, 4)], m1s, m1r, ((ctx + j) % 16, fsd)).start()
    pre_ctx = (2 * (y % 2) + c) * 4 + z
    pre_f = 2 * x + y // 2

    for n, src in enumerate((k, v)):
        dst = kvh.at[n, own_rows, :]
        for d in range(1, 4):
            t = (y + d) % 4
            rdma(src.at[:, pl.ds(pl.multiple_of(t * 256, 256), 256)], dst, kvs, kvr, y_dev(t)).start()
        pltpu.make_async_copy(src.at[:, pl.ds(pl.multiple_of(y * 256, 256), 256)], dst, kvr).start()

    def g_start(i, carry):
        cols = pl.ds(pl.multiple_of(i * 256, 256), 256)
        dst = gh.at[own_rows, cols]
        for d in range(1, 4):
            t = (y + d) % 4
            part = g.at[:, pl.ds(pl.multiple_of(t * 2048 + i * 256, 256), 256)]
            rdma(part, dst, qgs, qgr.at[i], y_dev(t)).start()
        part = g.at[:, pl.ds(pl.multiple_of(y * 2048 + i * 256, 256), 256)]
        pltpu.make_async_copy(part, dst, qgr.at[i]).start()
        return carry

    lax.fori_loop(0, EARLY, g_start, 0)
    await_on(m1, m1r)
    own_shard = pl.ds(pl.multiple_of(fsd * 16, 16), 16)

    def share(src, dst, ssem, rsem):
        pltpu.make_async_copy(src, dst, rsem).start()
        for d in range(1, 8):
            rdma(src, dst, ssem, rsem, (ctx, (fsd + d) % 8)).start()

    for t in range(8):
        mk2[t] = jnp.concatenate((m1[16 * y + 2 * t][:, FH:], m1[16 * y + 2 * t + 1][:, FH:]), axis=-1)
    share(mk2, mkp.at[:, own_shard, :], m2s, m2r)
    for t in range(32):
        mq2[t] = jnp.concatenate((m1[2 * t][:, :FH], m1[2 * t + 1][:, :FH]), axis=-1)
    share(mq2, mqa.at[:, own_shard, :], m3s, m3r)
    put(pst.at[pl.ds(2 * c, 2)], praw, ps.at[0], pr.at[0], pre_ctx, pre_f)
    put(nblk, pnr, ps.at[1], pr.at[1], pre_ctx, pre_f)
    await_on(kvh, kvr)
    ones = jnp.where(lax.broadcasted_iota(jnp.int32, (16, BLK), 0) == 0, 1.0, 0.0).astype(BF)
    for n in range(2):
        vt[n, 0:HD, :] = jnp.transpose(kvh[1, :, n * HD : (n + 1) * HD])
        vt[n, HD:EXL, :] = ones
    dvt[...] = jnp.zeros_like(dvt)
    dk[...] = jnp.zeros_like(dk)

    await_on(mkp, m2r)

    def r_dev(i):
        return ((i % 4) * 4 + y, 2 * x + i // 4)

    def to_owner(i, src, dst, ssem, rsem):
        dev = r_dev(i)
        put(src, dst.at[r], ssem, rsem, dev[0], dev[1])

    def keys_step(i, carry):
        n = i // 4
        cols = pl.ds(pl.multiple_of(n * HD, HD), HD)
        pair_t = jnp.transpose(mkp[i])
        mt[i] = pair_t
        logits = mm(pair_t, kvh[0, :, cols], 1, 1)
        for u in range(2):
            h = 2 * i + u
            pos, neg = soft_pair(logits[FH * u : FH * (u + 1)])
            both = jnp.concatenate((pos, neg), axis=0)
            kp[h] = both
            feat = both.astype(BF)
            kft[h] = feat
            feat_rows = jnp.transpose(feat)
            kf[h] = feat_rows
            sext[h] = low_ext(mm(vt[n], feat_rows))
        to_owner(i, sext.at[pl.ds(2 * i, 2)], rin, ss, sr)
        return carry

    lax.fori_loop(0, 8, keys_step, 0)

    def scan_out(parts, psem, tot, xsem_s, xsem_r):
        await_on(parts, psem)
        for u in range(2):
            total = wide_ext(parts[0, u])
            for j in range(1, 8):
                total = total + wide_ext(parts[j, u])
            tot[x, u] = low_ext(total)
        for d in range(1, 4):
            rdma(tot.at[x], tot.at[x], xsem_s, xsem_r, (ctx, 2 * ((x + d) % 4) + c)).start()

    def scan_back(parts, tot, xsem_r, outs, back, bsem_s, bsem_r, forward):
        if forward:
            await_on(praw, pr.at[0])
            await_on(pnr, pr.at[1])
            for u in range(2):
                acc[u, 0:HD] = jnp.transpose(praw[u])
                acc[u, HD:EXT] = pnr[u]
        else:
            acc[...] = jnp.zeros_like(acc)
        await_on(tot.at[pl.ds(0, 3)], xsem_r)
        for j in range(4):

            @pl.when((j < x) if forward else (j > x))
            def _():
                for u in range(2):
                    acc[u] += wide_ext(tot[j, u])

        run = [acc[0], acc[1]]
        for j in range(8) if forward else reversed(range(8)):
            for u in range(2):
                outs[j, u] = low_ext(run[u])
                run[u] = run[u] + wide_ext(parts[j, u])
            dev = r_dev(j)
            put(outs.at[j], back.at[pl.ds(2 * r, 2)], bsem_s, bsem_r.at[r], dev[0], dev[1])

    scan_out(rin, sr, xin, xs, xr)

    await_on(mqa, m3r)
    rows_in.wait()
    pltpu.make_async_copy(mqa, omq, loc.at[0]).start()

    def logits_step(i, carry):
        for t in range(4):
            p = 8 * t + i
            two = [qv[:, pl.ds(pl.multiple_of(p * 256 + e * HD, HD), HD)] for e in range(2)]
            res = mm(mqa[p], jnp.concatenate(two, axis=0), 0, 1).astype(BF)
            lts[p] = jnp.concatenate((res[:FH, :HD], res[FH:, HD:]), axis=0)
        dst = lq.at[i, :, pl.ds(pl.multiple_of(y * 128, 128), 128)]
        for d in range(1, 4):
            t = (y + d) % 4
            rdma(lts.at[8 * t + i], dst, lqs, lqr.at[i], y_dev(t)).start()
        pltpu.make_async_copy(lts.at[8 * y + i], dst, lqr.at[i]).start()

        @pl.when(i < 8 - EARLY)
        def _():
            g_start(i + EARLY, 0)

        return carry

    lax.fori_loop(0, 8, logits_step, 0)
    scan_back(rin, xin, xr, rout, stl, bs, br, True)

    ahead = lax.broadcasted_iota(jnp.int32, (BLK, BLK), 0) <= lax.broadcasted_iota(jnp.int32, (BLK, BLK), 1)

    def back_start(i):
        lanes = pl.ds(pl.multiple_of(i * 128, 128), 128)
        dst = dlv.at[:, pl.ds(pl.multiple_of(y * 1024 + i * 128, 128), 128)]
        for d in range(1, 4):
            t = (y + d) % 4
            rdma(dl.at[pl.ds(pl.multiple_of(t * 128, 128), 128), lanes], dst, oqs, oqr.at[i], y_dev(t)).start()
        pltpu.make_async_copy(dl.at[own_rows, lanes], dst, oqr.at[i]).start()

    def queries_first(i):
        n = i // 4
        await_on(stl.at[pl.ds(2 * i, 2)], br.at[i])
        await_on(lq.at[i], lqr.at[i])
        await_on(gh.at[:, pl.ds(pl.multiple_of(i * 256, 256), 256)], qgr.at[i])
        for u in range(2):
            h = 2 * i + u
            cols = pl.ds(pl.multiple_of(h * HD, HD), HD)
            pos, neg = soft_pair(lq[i, FH * u : FH * (u + 1), :])
            both = jnp.concatenate((pos, neg), axis=0)
            qp[h] = both
            qft = both.astype(BF)
            qf[h] = qft
            st = jnp.where(ahead, mm(kf[h], qft), 0.0)
            stlow = st.astype(BF)
            sts[h] = stlow
            inter = mm(stl[h], qft)
            num = inter[:HD] + mm(vt[n, 0:HD], stlow)
            den = (inter[HD : HD + 1] + inter[HD + 1 : HD + 2] + inter[HD + 2 : HD + 3]) + jnp.sum(
                st, axis=0, keepdims=True
            )
            inv = 1.0 / den
            sc = jnp.transpose(gh[:, cols]).astype(F32) * inv
            scl = sc.astype(BF)
            scs[h] = scl
            ng = -jnp.sum(sc * (num * inv), axis=0, keepdims=True)
            ngs[h] = ng
            part = mm(jnp.concatenate((scl, three_rows(ng, 16)), axis=0), qft, 1, 1)
            row = part[HD : HD + 1] + part[HD + 1 : HD + 2] + part[HD + 2 : HD + 3]
            uext[h] = jnp.concatenate((part[:HD].astype(BF), three_rows(row, 16)), axis=0)
        to_owner(i, uext.at[pl.ds(2 * i, 2)], uin, us, ur)

    def queries_second(i):
        n = i // 4
        vcols = pl.ds(pl.multiple_of(n * HD, HD), HD)
        logs = []
        for u in range(2):
            h = 2 * i + u
            scl = scs[h]
            ng = ngs[h]
            qft = qf[h]
            ext = stl[h]
            dst = jnp.where(ahead, mm(kvh[1, :, vcols], scl) + ng, 0.0).astype(BF)
            dfq = mm(ext[:HD], scl, 0, 0) + norm_column(ext) * ng + mm(kft[h], dst)
            dfk[h] = mm(qft, dst, 1, 1)
            dvt[n] += mm(scl, sts[h], 1, 1)
            both = qp[h]
            dlt = soft_back(both[:FH], both[FH:], dfq)
            logs.append(dlt)
        dl[:, pl.ds(pl.multiple_of(i * 128, 128), 128)] = jnp.transpose(jnp.concatenate(logs, axis=0))
        back_start(i)

    def map_step(i):
        await_on(dlv.at[:, pl.ds(0, 512)], oqr.at[i])
        for t in range(4):
            p = 8 * t + i
            res = mm(
                dlv[:, pl.ds(pl.multiple_of(p * 128, 128), 128)],
                qv[:, pl.ds(pl.multiple_of(p * 256, 256), 256)], 0, 0,
            ).astype(BF)
            gqs[i, t] = jnp.concatenate((res[:FH, :HD], res[FH:, HD:]), axis=0)
        to_owner(i, gqs.at[i], rq, rqs, rqr)

    def queries_step(t, carry):
        @pl.when(t < 8)
        def _():
            queries_first(t)

        @pl.when(t >= LAG)
        def _():
            queries_second(t - LAG)

        @pl.when(t >= LAG + MAP)
        def _():
            map_step(t - LAG - MAP)

        @pl.when(t == OUT)
        def _():
            scan_out(uin, ur, yin, ys, yr)

        @pl.when(t == BACK)
        def _():
            scan_back(uin, yin, yr, uout, sul, cs, cr, False)

        return carry

    lax.fori_loop(0, 8 + LAG, queries_step, 0)

    for u in range(2):
        whole = yin[0, u, :HD].astype(F32)
        for j in range(1, 4):
            whole = whole + yin[j, u, :HD].astype(F32)
        pgs[u] = jnp.transpose(whole)
    own_ctx = y * 4 + r // 2
    half = pl.ds(2 * (r % 2), 2)
    for e in range(2):
        put(
            pgs.at[:, pl.ds(pl.multiple_of((2 * x + e) * 16, 16), 16), :], op.at[half],
            gs, gr, own_ctx, 2 * x + e,
        )

    def kv_start(n):
        cols = pl.ds(pl.multiple_of(n * HD, HD), HD)
        for s, out in enumerate((ok, ov)):
            dst = out.at[:, pl.ds(pl.multiple_of(y * 256 + n * HD, HD), HD)]
            for d in range(1, 4):
                t = (y + d) % 4
                part = gkv.at[s, pl.ds(pl.multiple_of(t * 128, 128), 128), cols]
                rdma(part, dst, kos, kor.at[s], y_dev(t)).start()
            pltpu.make_async_copy(gkv.at[s, own_rows, cols], dst, kor.at[s]).start()

    def summed(src):
        total = src(0).astype(F32)
        for j in range(1, 8):
            total = total + src(j).astype(F32)
        return jnp.transpose(total).astype(BF)

    def queries_out():
        await_on(rq, rqr)
        for t in range(4):
            lowq[t] = summed(lambda j: rq[j, t])
            for e in range(8):
                to = (fsd + e) % 8
                put(
                    lowq.at[t, pl.ds(pl.multiple_of(to * 16, 16), 16), :], fq.at[x, y, r % 2],
                    fqs, fqr, t * 4 + r // 2, to,
                )

    def finish_step(i, carry):

        @pl.when(jnp.logical_and(i >= LATE, i < LATE + MAP))
        def _():
            map_step(i - LATE + 8 - MAP)

        @pl.when(i == LATE + MAP + 1)
        def _():
            queries_out()

        n = i // 4
        cols = pl.ds(pl.multiple_of(n * HD, HD), HD)
        await_on(sul.at[pl.ds(2 * i, 2)], cr.at[i])
        logs = []
        for u in range(2):
            h = 2 * i + u
            suf = sul[h]
            up = dfk[h] + mm(suf[:HD], vt[n, 0:HD], 0, 0) + norm_column(suf)
            dvt[n] += mm(suf[:HD], kft[h])
            both = kp[h]
            logs.append(soft_back(both[:FH], both[FH:], up))
        pair = jnp.concatenate(logs, axis=0)
        dk[n] += mm(jnp.transpose(pair), mt[i])
        gks[i] = mm(pair, kvh[0, :, cols]).astype(BF)
        to_owner(i, gks.at[i], rk, rks, rkr)

        @pl.when(i % 4 == 3)
        def _():
            gkv[0, :, cols] = dk[n].astype(BF)
            gkv[1, :, cols] = jnp.transpose(dvt[n]).astype(BF)
            kv_start(n)

        return carry

    lax.fori_loop(0, 8, finish_step, 0)
    if LATE + MAP + 1 > 7:
        queries_out()

    logs_out = pltpu.make_async_copy(dlv, odl, loc.at[1])
    logs_out.start()

    await_on(rk, rkr)
    lowk[...] = summed(lambda j: rk[j])
    for e in range(8):
        to = (fsd + e) % 8
        put(
            lowk.at[pl.ds(pl.multiple_of(to * 16, 16), 16), :], fk.at[x, r % 2],
            fks, fkr, own_ctx, to,
        )
    await_on(fq, fqr)
    for e in range(2):
        total = fq[0, 0, e].astype(F32)
        for j in range(1, 16):
            total = total + fq[j // 4, j % 4, e].astype(F32)
        fmo[0, e] = total
    await_on(fk, fkr)
    for e in range(2):
        fmo[1, e] = (fk[0, e].astype(F32) + fk[1, e].astype(F32)) + (fk[2, e].astype(F32) + fk[3, e].astype(F32))
    last = pltpu.make_async_copy(fmo, om, loc.at[2])
    last.start()

    await_on(op, gr)
    here = own_ctx == ctx

    @pl.when(here)
    def _():
        await_on(op.at[pl.ds(0, 2)], gs)
        await_on(m1.at[pl.ds(0, 7)], fks)

    @pl.when(jnp.logical_not(here))
    def _():
        await_on(op, gs)
        await_on(m1.at[pl.ds(0, 8)], fks)

    @pl.when(r // 2 == y)
    def _():
        await_on(m1.at[pl.ds(0, 31)], fqs)

    @pl.when(r // 2 != y)
    def _():
        await_on(m1.at[pl.ds(0, 32)], fqs)

    await_on(xin.at[pl.ds(0, 3)], xs)
    await_on(yin.at[pl.ds(0, 3)], ys)
    await_on(m1.at[pl.ds(0, 60)], m1s)
    sent(praw, ps.at[0], pre_ctx, pre_f)
    sent(pnr, ps.at[1], pre_ctx, pre_f)
    await_on(mkp.at[:, pl.ds(0, 112), :], m2s)
    await_on(mqa.at[:, pl.ds(0, 112), :], m3s)
    await_on(mqa, loc.at[0])
    await_on(kvh.at[:, pl.ds(0, 384), :], kvs)
    await_on(gh.at[pl.ds(0, 384), :], qgs)
    await_on(lts.at[pl.ds(0, 24)], lqs)
    await_on(dl.at[pl.ds(0, 384), :], oqs)
    await_on(gkv.at[:, pl.ds(0, 384), :], kos)
    await_on(ok, kor.at[0])
    await_on(ov, kor.at[1])
    for sem in (ss, us):
        await_on(rin.at[pl.ds(0, 7)], sem)
    for sem in (bs, cs):
        await_on(rout.at[pl.ds(0, 7)], sem)
    await_on(rq.at[pl.ds(0, 7)], rqs)
    await_on(rk.at[pl.ds(0, 7)], rks)
    logs_out.wait()
    last.wait()


def close(dl, mq, k, v, m, p, oq, ok, ov, omq, omk, op):
    i = pl.program_id(0)
    lane = lax.broadcasted_iota(jnp.int32, (HD, HD), 1)
    for t in range(8):
        pair = mq[t]
        zero = jnp.zeros_like(pair)
        wide = jnp.concatenate((jnp.where(lane < FH, pair, zero), jnp.where(lane < FH, zero, pair)), axis=0)
        oq[:, 2 * t * HD : 2 * (t + 1) * HD] = mm(dl[:, t * HD : (t + 1) * HD], wide, 1, 1).astype(BF)

    ok[...] = k[...]
    ov[...] = v[...]

    @pl.when(i == 0)
    def _():
        for h in range(4):
            omq[h] = m[0, h // 2, :, FH * (h % 2) : FH * (h % 2 + 1)]
            omk[h] = m[1, h // 2, :, FH * (h % 2) : FH * (h % 2 + 1)]
        op[...] = p[...]


def shards(query_rows, key_rows, value_rows, grad_out, query_map, key_map, prefix_state, prefix_norm):
    dma = lambda *s: pltpu.SemaphoreType.DMA(s)
    vm = lambda dt, *s: pltpu.VMEM(s, dt)
    outs = pl.pallas_call(
        kernel,
        out_shape=(
            jax.ShapeDtypeStruct((128, 4096), BF),
            jax.ShapeDtypeStruct((32, 128, 128), BF),
            jax.ShapeDtypeStruct((128, 1024), BF),
            jax.ShapeDtypeStruct((128, 1024), BF),
            jax.ShapeDtypeStruct((2, 2, 16, 128), F32),
            jax.ShapeDtypeStruct((4, 16, 128), F32),
        ),
        in_specs=[pl.BlockSpec(memory_space=pl.ANY)] * 8,
        out_specs=[pl.BlockSpec(memory_space=pl.ANY)] * 6,
        scratch_shapes=[
            vm(BF, 4, 16, 64), vm(BF, 4, 16, 64), vm(F32, 4, 128), vm(BF, 4, 16, 128), vm(F32, 2, 8, 128),
            vm(BF, 64, 16, 128), vm(BF, 8, 16, 128), vm(BF, 32, 16, 128),
            vm(BF, 8, 128, 128), vm(BF, 32, 128, 128), vm(BF, 8, 128, 128),
            vm(BF, 128, 8192), vm(BF, 32, 128, 128), vm(BF, 8, 128, 512),
            vm(BF, 512, 2048), vm(BF, 2, 512, 256),
            vm(BF, 2, EXL, 512), vm(BF, 16, 512, 128), vm(BF, 16, 128, 512), vm(F32, 16, 128, 512),
            vm(BF, 16, EXL, 128), vm(BF, 16, EXL, 128),
            vm(BF, 8, 2, EXL, 128), vm(BF, 8, 2, EXL, 128),
            vm(BF, 4, 2, EXL, 128), vm(BF, 4, 2, EXL, 128), vm(F32, 2, 128, 128), vm(F32, 2, 8, 128),
            vm(BF, 8, 2, EXL, 128), vm(BF, 8, 2, EXL, 128),
            vm(BF, 16, EXL, 128), vm(BF, 16, EXL, 128),
            vm(F32, 16, 128, 512), vm(F32, 2, 128, 512), vm(F32, 2, 512, 128),
            vm(F32, 16, 128, 512), vm(BF, 16, 128, 512), vm(BF, 16, 512, 512), vm(BF, 16, 128, 512), vm(F32, 16, 1, 512),
            vm(BF, 512, 1024), vm(BF, 128, 4096), vm(BF, 8, 4, 128, 128), vm(BF, 8, 4, 128, 128),
            vm(BF, 8, 128, 128), vm(BF, 8, 128, 128), vm(BF, 4, 128, 128), vm(BF, 128, 128),
            vm(BF, 4, 4, 2, 16, 128), vm(BF, 4, 2, 16, 128), vm(F32, 2, 2, 16, 128), vm(F32, 2, 128, 128),
            vm(BF, 2, 512, 256), vm(F32, 2, EXT, 128),
            dma(), dma(), dma(), dma(), dma(), dma(), dma(2), dma(2), dma(), dma(), dma(), dma(8), dma(), dma(8), dma(4),
            dma(), dma(), dma(), dma(), dma(), dma(8), dma(), dma(), dma(), dma(), dma(), dma(8), dma(), dma(8), dma(), dma(2),
            dma(), dma(), dma(), dma(), dma(), dma(), dma(), dma(), dma(), dma(),
        ],
        compiler_params=pltpu.CompilerParams(
            collective_id=0, has_side_effects=True, vmem_limit_bytes=60 * 1024 * 1024
        ),
    )(query_map, key_map, prefix_state, prefix_norm, query_rows, grad_out, key_rows, value_rows)
    log_q, map_q, grad_k, grad_v, grad_m, grad_p = outs
    whole = lambda *s: pl.BlockSpec(s, lambda i: (0,) * len(s))
    return pl.pallas_call(
        close,
        grid=(4,),
        out_shape=(
            jax.ShapeDtypeStruct((128, 8192), BF),
            jax.ShapeDtypeStruct((128, 1024), BF),
            jax.ShapeDtypeStruct((128, 1024), BF),
            jax.ShapeDtypeStruct((4, 16, 64), F32),
            jax.ShapeDtypeStruct((4, 16, 64), F32),
            jax.ShapeDtypeStruct((4, 16, 128), F32),
        ),
        in_specs=[
            pl.BlockSpec((128, 1024), lambda i: (0, i)),
            pl.BlockSpec((8, 128, 128), lambda i: (i, 0, 0)),
            pl.BlockSpec((128, 256), lambda i: (0, i)),
            pl.BlockSpec((128, 256), lambda i: (0, i)),
            whole(2, 2, 16, 128),
            whole(4, 16, 128),
        ],
        out_specs=[
            pl.BlockSpec((128, 2048), lambda i: (0, i)),
            pl.BlockSpec((128, 256), lambda i: (0, i)),
            pl.BlockSpec((128, 256), lambda i: (0, i)),
            whole(4, 16, 64),
            whole(4, 16, 64),
            whole(4, 16, 128),
        ],
    )(log_q, map_q, grad_k, grad_v, grad_m, grad_p)


def solution(mesh):
    both = ("fsdp", "ctx")
    rows = P(both, None)
    return jax.shard_map(
        shards,
        mesh=mesh,
        in_specs=(
            rows, rows, rows, rows,
            P("ctx", "fsdp", None), P("ctx", "fsdp", None),
            P("ctx", None, None), P("ctx", None),
        ),
        out_specs=(
            rows, rows, rows,
            P("ctx", "fsdp", None), P("ctx", "fsdp", None), P("ctx", "fsdp", None),
        ),
        check_vma=False,
    )
```

```python
import functools

import jax
import jax.numpy as jnp
from jax import lax
from jax.experimental import pallas as pl
from jax.experimental.pallas import tpu as pltpu
from jax.sharding import PartitionSpec as P

HD = 128
FH = 64
BLK = 512
EXT = 136
EXL = 144
HALF = 256
LAG = 8
THIRD = 8
OUT = 8
BACK = 13
EARLY = 5
MAP = 8
EARLIER = 5
LATE = 1
QOUT = 8
MESH = pl.DeviceIdType.MESH
F32 = jnp.float32
BF = jnp.bfloat16


def mm(a, b, ca=1, cb=0):
    return lax.dot_general(a, b, (((ca,), (cb,)), ((), ())), preferred_element_type=F32)


def soft_pair(logits):
    wide = logits.astype(BF).astype(F32)
    up = jnp.exp(wide)
    low = jnp.exp(-wide)
    pos = up * (1.0 / jnp.sum(up, axis=0, keepdims=True))
    neg = low * (1.0 / jnp.sum(low, axis=0, keepdims=True))
    return pos, neg


def soft_back(pos, neg, up):
    one = up[:FH]
    two = up[FH:]
    first = pos * (one - jnp.sum(pos * one, axis=0, keepdims=True))
    second = neg * (two - jnp.sum(neg * two, axis=0, keepdims=True))
    return (first - second).astype(BF)


def three_rows(row, height):
    high = row.astype(BF).astype(F32)
    rest = row - high
    mid = rest.astype(BF).astype(F32)
    last = rest - mid
    at = lax.broadcasted_iota(jnp.int32, (height, row.shape[1]), 0)
    zero = jnp.zeros((height, row.shape[1]), F32)
    out = jnp.where(at == 0, high, jnp.where(at == 1, mid, jnp.where(at == 2, last, zero)))
    return out.astype(BF)


def low_ext(wide):
    return jnp.concatenate((wide[:HD].astype(BF), three_rows(wide[HD : HD + 1], 16)), axis=0)


def wide_ext(low):
    tail = low[HD:EXL].astype(F32)
    row = tail[0:1] + tail[1:2] + tail[2:3]
    return jnp.concatenate((low[:HD].astype(F32), jnp.broadcast_to(row, (8, HD))), axis=0)


def norm_column(low):
    tail = low[HD:EXL].astype(F32)
    row = tail[0:1] + tail[1:2] + tail[2:3]
    return jnp.transpose(jnp.broadcast_to(row, (8, HD)))[:, 0:1]


def kernel(
    qmap, kmap, pst, pnm, q, g, k, v,
    odl, omq, ok, ov, om, op,
    qin, kin, nin, maps, nblk, m1, mk2, mq2, mkp, mqa, mt, qv, lts, lq, gh, kvh, vt, kf, kft, kp,
    sext, uext, rin, uin, xin, yin, praw, pnr, rout, uout, stl, sul,
    dfk, dvt, dk, qp, qf, sts, dss, scs, ngs, dl, dlv, gqs, rq, gks, rk, lowq, lowk, fq, fk, fmo, pgs, gkv, acc,
    m1s, m1r, m2s, m2r, m3s, m3r, ps, pr, kvs, kvr, qgs, qgr, lqs, lqr, loc,
    ss, sr, xs, xr, bs, br, us, ur, ys, yr, cs, cr, oqs, oqr, kos, kor,
    rqs, rqr, rks, rkr, fqs, fqr, fks, fkr, gs, gr,
):
    ctx = lax.axis_index("ctx")
    fsd = lax.axis_index("fsdp")
    z = ctx // 4
    y = ctx % 4
    x = fsd // 2
    c = fsd % 2
    r = c * 4 + z

    def rdma(src, dst, ssem, rsem, dev):
        return pltpu.make_async_remote_copy(
            src_ref=src, dst_ref=dst, send_sem=ssem, recv_sem=rsem, device_id=dev, device_id_type=MESH
        )

    def await_on(ref, sem):
        pltpu.make_async_copy(ref, ref, sem).wait()

    first = [
        pltpu.make_async_copy(qmap, qin, loc.at[0]),
        pltpu.make_async_copy(kmap, kin, loc.at[1]),
        pltpu.make_async_copy(pnm, nin, loc.at[2]),
    ]
    for copy in first:
        copy.start()
    rows_in = pltpu.make_async_copy(q, qv, loc.at[3])
    rows_in.start()
    other = fsd + 1 - 2 * c
    barrier = pltpu.get_barrier_semaphore()
    for j in range(1, 8):
        pl.semaphore_signal(barrier, inc=1, device_id=(ctx, (fsd + j) % 8), device_id_type=MESH)

    def greet(j, carry):
        at = (ctx + j) % 16
        for e in range(4):
            pl.semaphore_signal(barrier, inc=1, device_id=(at, 2 * e + c), device_id_type=MESH)
            pl.semaphore_signal(barrier, inc=1, device_id=(at, 2 * e + 1 - c), device_id_type=MESH)
        return carry

    lax.fori_loop(1, 16, greet, 0)
    for copy in first:
        copy.wait()
    maps[...] = jnp.concatenate((qin[...], kin[...]), axis=-1)
    norms = jnp.where(c == 0, nin[0:2, :], nin[2:4, :])
    for u in range(2):
        nblk[u] = jnp.broadcast_to(norms[u : u + 1], (8, HD))
    pl.semaphore_wait(barrier, 127)

    def y_dev(t):
        return (z * 4 + t, fsd)

    own_rows = pl.ds(y * 128, 128)

    def put(src, dst, ssem, rsem, dev_ctx, dev_f):
        is_me = jnp.logical_and(dev_ctx == ctx, dev_f == fsd)

        @pl.when(is_me)
        def _():
            pltpu.make_async_copy(src, dst, rsem).start()

        @pl.when(jnp.logical_not(is_me))
        def _():
            rdma(src, dst, ssem, rsem, (dev_ctx, dev_f)).start()

    def sent(src, ssem, dev_ctx, dev_f):
        is_me = jnp.logical_and(dev_ctx == ctx, dev_f == fsd)

        @pl.when(jnp.logical_not(is_me))
        def _():
            await_on(src, ssem)

    pltpu.make_async_copy(maps, m1.at[pl.ds(4 * ctx, 4)], m1r).start()
    for j in range(1, 16):
        rdma(maps, m1.at[pl.ds(4 * ctx, 4)], m1s, m1r, ((ctx + j) % 16, fsd)).start()
    pre_ctx = (2 * (y % 2) + c) * 4 + z
    pre_f = 2 * x + y // 2

    for n, src in enumerate((k, v)):
        dst = kvh.at[n, own_rows, :]
        for d in range(1, 4):
            t = (y + d) % 4
            rdma(src.at[:, pl.ds(pl.multiple_of(t * 256, 256), 256)], dst, kvs, kvr, y_dev(t)).start()
        pltpu.make_async_copy(src.at[:, pl.ds(pl.multiple_of(y * 256, 256), 256)], dst, kvr).start()

    def g_start(i, carry):
        cols = pl.ds(pl.multiple_of(i * 256, 256), 256)
        dst = gh.at[own_rows, cols]
        for d in range(1, 4):
            t = (y + d) % 4
            part = g.at[:, pl.ds(pl.multiple_of(t * 2048 + i * 256, 256), 256)]
            rdma(part, dst, qgs, qgr.at[i], y_dev(t)).start()
        part = g.at[:, pl.ds(pl.multiple_of(y * 2048 + i * 256, 256), 256)]
        pltpu.make_async_copy(part, dst, qgr.at[i]).start()
        return carry

    lax.fori_loop(0, EARLY, g_start, 0)
    await_on(m1, m1r)
    own_shard = pl.ds(pl.multiple_of(fsd * 16, 16), 16)

    def share(src, dst, ssem, rsem):
        pltpu.make_async_copy(src, dst, rsem).start()
        for d in range(1, 8):
            rdma(src, dst, ssem, rsem, (ctx, (fsd + d) % 8)).start()

    for t in range(8):
        mk2[t] = jnp.concatenate((m1[16 * y + 2 * t][:, FH:], m1[16 * y + 2 * t + 1][:, FH:]), axis=-1)
    share(mk2, mkp.at[:, own_shard, :], m2s, m2r)
    for t in range(32):
        mq2[t] = jnp.concatenate((m1[2 * t][:, :FH], m1[2 * t + 1][:, :FH]), axis=-1)
    share(mq2, mqa.at[:, own_shard, :], m3s, m3r)
    put(pst.at[pl.ds(2 * c, 2)], praw, ps.at[0], pr.at[0], pre_ctx, pre_f)
    put(nblk, pnr, ps.at[1], pr.at[1], pre_ctx, pre_f)
    await_on(kvh, kvr)
    ones = jnp.where(lax.broadcasted_iota(jnp.int32, (16, BLK), 0) == 0, 1.0, 0.0).astype(BF)
    for n in range(2):
        vt[n, 0:HD, :] = jnp.transpose(kvh[1, :, n * HD : (n + 1) * HD])
        vt[n, HD:EXL, :] = ones
    dvt[...] = jnp.zeros_like(dvt)
    dk[...] = jnp.zeros_like(dk)

    await_on(mkp, m2r)

    def r_dev(i):
        return ((i % 4) * 4 + y, 2 * x + i // 4)

    def to_owner(i, src, dst, ssem, rsem):
        dev = r_dev(i)
        put(src, dst.at[r], ssem, rsem, dev[0], dev[1])

    def keys_step(i, carry):
        n = i // 4
        cols = pl.ds(pl.multiple_of(n * HD, HD), HD)
        pair_t = jnp.transpose(mkp[i])
        mt[i] = pair_t
        logits = mm(pair_t, kvh[0, :, cols], 1, 1)
        for u in range(2):
            h = 2 * i + u
            pos, neg = soft_pair(logits[FH * u : FH * (u + 1)])
            both = jnp.concatenate((pos, neg), axis=0)
            kp[h] = both
            feat = both.astype(BF)
            kft[h] = feat
            feat_rows = jnp.transpose(feat)
            kf[h] = feat_rows
            sext[h] = low_ext(mm(vt[n], feat_rows))
        to_owner(i, sext.at[pl.ds(2 * i, 2)], rin, ss, sr)
        return carry

    lax.fori_loop(0, 8, keys_step, 0)

    def scan_out(parts, psem, tot, xsem_s, xsem_r):
        await_on(parts, psem)
        for u in range(2):
            total = wide_ext(parts[0, u])
            for j in range(1, 8):
                total = total + wide_ext(parts[j, u])
            tot[x, u] = low_ext(total)
        for d in range(1, 4):
            rdma(tot.at[x], tot.at[x], xsem_s, xsem_r, (ctx, 2 * ((x + d) % 4) + c)).start()

    def scan_back(parts, tot, xsem_r, outs, back, bsem_s, bsem_r, forward):
        if forward:
            await_on(praw, pr.at[0])
            await_on(pnr, pr.at[1])
            for u in range(2):
                acc[u, 0:HD] = jnp.transpose(praw[u])
                acc[u, HD:EXT] = pnr[u]
        else:
            acc[...] = jnp.zeros_like(acc)
        await_on(tot.at[pl.ds(0, 3)], xsem_r)
        for j in range(4):

            @pl.when((j < x) if forward else (j > x))
            def _():
                for u in range(2):
                    acc[u] += wide_ext(tot[j, u])

        run = [acc[0], acc[1]]
        for j in range(8) if forward else reversed(range(8)):
            for u in range(2):
                outs[j, u] = low_ext(run[u])
                run[u] = run[u] + wide_ext(parts[j, u])
            dev = r_dev(j)
            put(outs.at[j], back.at[pl.ds(2 * r, 2)], bsem_s, bsem_r.at[r], dev[0], dev[1])

    scan_out(rin, sr, xin, xs, xr)

    await_on(mqa, m3r)
    rows_in.wait()
    pltpu.make_async_copy(mqa, omq, loc.at[0]).start()

    def logits_step(i, carry):
        for t in range(4):
            p = 8 * t + i
            two = [qv[:, pl.ds(pl.multiple_of(p * 256 + e * HD, HD), HD)] for e in range(2)]
            res = mm(mqa[p], jnp.concatenate(two, axis=0), 0, 1).astype(BF)
            lts[p] = jnp.concatenate((res[:FH, :HD], res[FH:, HD:]), axis=0)
        dst = lq.at[i, :, pl.ds(pl.multiple_of(y * 128, 128), 128)]
        for d in range(1, 4):
            t = (y + d) % 4
            rdma(lts.at[8 * t + i], dst, lqs, lqr.at[i], y_dev(t)).start()
        pltpu.make_async_copy(lts.at[8 * y + i], dst, lqr.at[i]).start()

        @pl.when(i < 8 - EARLY)
        def _():
            g_start(i + EARLY, 0)

        return carry

    lax.fori_loop(0, 8, logits_step, 0)
    scan_back(rin, xin, xr, rout, stl, bs, br, True)

    ahead = lax.broadcasted_iota(jnp.int32, (HALF, HALF), 0) <= lax.broadcasted_iota(jnp.int32, (HALF, HALF), 1)

    def back_start(i):
        lanes = pl.ds(pl.multiple_of(i * 128, 128), 128)
        dst = dlv.at[:, pl.ds(pl.multiple_of(y * 1024 + i * 128, 128), 128)]
        for d in range(1, 4):
            t = (y + d) % 4
            rdma(dl.at[pl.ds(pl.multiple_of(t * 128, 128), 128), lanes], dst, oqs, oqr.at[i], y_dev(t)).start()
        pltpu.make_async_copy(dl.at[own_rows, lanes], dst, oqr.at[i]).start()

    def queries_first(i):
        n = i // 4
        await_on(stl.at[pl.ds(2 * i, 2)], br.at[i])
        await_on(lq.at[i], lqr.at[i])
        await_on(gh.at[:, pl.ds(pl.multiple_of(i * 256, 256), 256)], qgr.at[i])
        for u in range(2):
            h = 2 * i + u
            cols = pl.ds(pl.multiple_of(h * HD, HD), HD)
            pos, neg = soft_pair(lq[i, FH * u : FH * (u + 1), :])
            both = jnp.concatenate((pos, neg), axis=0)
            qp[h] = both
            qft = both.astype(BF)
            qf[h] = qft
            st0 = jnp.where(ahead, mm(kf[h, 0:HALF], qft[:, :HALF]), 0.0)
            st1 = mm(kf[h], qft[:, HALF:])
            st2 = jnp.where(ahead, st1[HALF:], 0.0)
            st1 = st1[:HALF]
            low0, low1, low2 = (part.astype(BF) for part in (st0, st1, st2))
            sts[h, 0:HALF, 0:HALF] = low0
            sts[h, 0:HALF, HALF:BLK] = low1
            sts[h, HALF:BLK, HALF:BLK] = low2
            inter = mm(stl[h], qft)
            own = jnp.concatenate(
                (mm(vt[n, 0:HD, 0:HALF], low0), mm(vt[n, 0:HD], jnp.concatenate((low1, low2), axis=0))), axis=1
            )
            num = inter[:HD] + own
            sums = jnp.concatenate(
                (jnp.sum(st0, axis=0, keepdims=True), jnp.sum(st1 + st2, axis=0, keepdims=True)), axis=1
            )
            den = (inter[HD : HD + 1] + inter[HD + 1 : HD + 2] + inter[HD + 2 : HD + 3]) + sums
            inv = 1.0 / den
            sc = jnp.transpose(gh[:, cols]).astype(F32) * inv
            scl = sc.astype(BF)
            scs[h] = scl
            ng = -jnp.sum(sc * (num * inv), axis=0, keepdims=True)
            ngs[h] = ng
            part = mm(jnp.concatenate((scl, three_rows(ng, 16)), axis=0), qft, 1, 1)
            row = part[HD : HD + 1] + part[HD + 1 : HD + 2] + part[HD + 2 : HD + 3]
            uext[h] = jnp.concatenate((part[:HD].astype(BF), three_rows(row, 16)), axis=0)
        to_owner(i, uext.at[pl.ds(2 * i, 2)], uin, us, ur)

    def queries_second(i):
        n = i // 4
        vcols = pl.ds(pl.multiple_of(n * HD, HD), HD)
        logs = []
        for u in range(2):
            h = 2 * i + u
            scl = scs[h]
            ng = ngs[h]
            ext = stl[h]
            value = kvh[1, :, vcols]
            ds0 = jnp.where(ahead, mm(value[:HALF], scl[:, :HALF]) + ng[:, :HALF], 0.0).astype(BF)
            ds1 = mm(value, scl[:, HALF:]) + ng[:, HALF:]
            ds2 = jnp.where(ahead, ds1[HALF:], 0.0).astype(BF)
            ds1 = ds1[:HALF].astype(BF)
            dss[h, 0:HALF, 0:HALF] = ds0
            dss[h, 0:HALF, HALF:BLK] = ds1
            dss[h, HALF:BLK, HALF:BLK] = ds2
            own = jnp.concatenate(
                (mm(kft[h, :, 0:HALF], ds0), mm(kft[h], jnp.concatenate((ds1, ds2), axis=0))), axis=1
            )
            dfq = mm(ext[:HD], scl, 0, 0) + norm_column(ext) * ng + own
            both = qp[h]
            dlt = soft_back(both[:FH], both[FH:], dfq)
            logs.append(dlt)
        dl[:, pl.ds(pl.multiple_of(i * 128, 128), 128)] = jnp.transpose(jnp.concatenate(logs, axis=0))
        back_start(i)

    def queries_third(i):
        n = i // 4
        for u in range(2):
            h = 2 * i + u
            early = mm(qf[h], dss[h, 0:HALF, :], 1, 1)
            late = mm(qf[h, :, HALF:BLK], dss[h, HALF:BLK, HALF:BLK], 1, 1)
            dfk[h] = jnp.concatenate((early, late), axis=1)
            early = mm(scs[h], sts[h, 0:HALF, :], 1, 1)
            late = mm(scs[h, :, HALF:BLK], sts[h, HALF:BLK, HALF:BLK], 1, 1)
            dvt[n] += jnp.concatenate((early, late), axis=1)

    def map_step(i):
        await_on(dlv.at[:, pl.ds(0, 512)], oqr.at[i])
        for t in range(4):
            p = 8 * t + i
            res = mm(
                dlv[:, pl.ds(pl.multiple_of(p * 128, 128), 128)],
                qv[:, pl.ds(pl.multiple_of(p * 256, 256), 256)], 0, 0,
            ).astype(BF)
            gqs[i, t] = jnp.concatenate((res[:FH, :HD], res[FH:, HD:]), axis=0)
        to_owner(i, gqs.at[i], rq, rqs, rqr)

    def queries_step(t, carry):
        @pl.when(t < 8)
        def _():
            queries_first(t)

        @pl.when(jnp.logical_and(t >= LAG, t < LAG + 8))
        def _():
            queries_second(t - LAG)

        @pl.when(t >= LAG + THIRD)
        def _():
            queries_third(t - LAG - THIRD)

        @pl.when(jnp.logical_and(t >= LAG + MAP, t < LAG + MAP + EARLIER))
        def _():
            map_step(t - LAG - MAP)

        @pl.when(t == OUT)
        def _():
            scan_out(uin, ur, yin, ys, yr)

        @pl.when(t == BACK)
        def _():
            scan_back(uin, yin, yr, uout, sul, cs, cr, False)

        return carry

    lax.fori_loop(0, 8 + LAG + THIRD, queries_step, 0)

    for u in range(2):
        whole = yin[0, u, :HD].astype(F32)
        for j in range(1, 4):
            whole = whole + yin[j, u, :HD].astype(F32)
        pgs[u] = jnp.transpose(whole)
    own_ctx = y * 4 + r // 2
    half = pl.ds(2 * (r % 2), 2)
    for e in range(2):
        put(
            pgs.at[:, pl.ds(pl.multiple_of((2 * x + e) * 16, 16), 16), :], op.at[half],
            gs, gr, own_ctx, 2 * x + e,
        )

    def kv_start(n):
        cols = pl.ds(pl.multiple_of(n * HD, HD), HD)
        for s, out in enumerate((ok, ov)):
            dst = out.at[:, pl.ds(pl.multiple_of(y * 256 + n * HD, HD), HD)]
            for d in range(1, 4):
                t = (y + d) % 4
                part = gkv.at[s, pl.ds(pl.multiple_of(t * 128, 128), 128), cols]
                rdma(part, dst, kos, kor.at[s], y_dev(t)).start()
            pltpu.make_async_copy(gkv.at[s, own_rows, cols], dst, kor.at[s]).start()

    def summed(src):
        total = src(0).astype(F32)
        for j in range(1, 8):
            total = total + src(j).astype(F32)
        return jnp.transpose(total).astype(BF)

    def queries_out():
        await_on(rq, rqr)
        for t in range(4):
            lowq[t] = summed(lambda j: rq[j, t])
            for e in range(8):
                to = (fsd + e) % 8
                put(
                    lowq.at[t, pl.ds(pl.multiple_of(to * 16, 16), 16), :], fq.at[x, y, r % 2],
                    fqs, fqr, t * 4 + r // 2, to,
                )

    def finish_step(i, carry):

        @pl.when(jnp.logical_and(i >= LATE, i < LATE + 8 - EARLIER))
        def _():
            map_step(i - LATE + EARLIER)

        @pl.when(i == QOUT)
        def _():
            queries_out()

        n = i // 4
        cols = pl.ds(pl.multiple_of(n * HD, HD), HD)
        await_on(sul.at[pl.ds(2 * i, 2)], cr.at[i])
        logs = []
        for u in range(2):
            h = 2 * i + u
            suf = sul[h]
            up = dfk[h] + mm(suf[:HD], vt[n, 0:HD], 0, 0) + norm_column(suf)
            dvt[n] += mm(suf[:HD], kft[h])
            both = kp[h]
            logs.append(soft_back(both[:FH], both[FH:], up))
        pair = jnp.concatenate(logs, axis=0)
        dk[n] += mm(jnp.transpose(pair), mt[i])
        gks[i] = mm(pair, kvh[0, :, cols]).astype(BF)
        to_owner(i, gks.at[i], rk, rks, rkr)

        @pl.when(i % 4 == 3)
        def _():
            gkv[0, :, cols] = dk[n].astype(BF)
            gkv[1, :, cols] = jnp.transpose(dvt[n]).astype(BF)
            kv_start(n)

        return carry

    lax.fori_loop(0, 8, finish_step, 0)
    if QOUT > 7:
        queries_out()

    logs_out = pltpu.make_async_copy(dlv, odl, loc.at[1])
    logs_out.start()

    await_on(rk, rkr)
    lowk[...] = summed(lambda j: rk[j])
    for e in range(8):
        to = (fsd + e) % 8
        put(
            lowk.at[pl.ds(pl.multiple_of(to * 16, 16), 16), :], fk.at[x, r % 2],
            fks, fkr, own_ctx, to,
        )
    await_on(fq, fqr)
    for e in range(2):
        total = fq[0, 0, e].astype(F32)
        for j in range(1, 16):
            total = total + fq[j // 4, j % 4, e].astype(F32)
        fmo[0, e] = total
    await_on(fk, fkr)
    for e in range(2):
        fmo[1, e] = (fk[0, e].astype(F32) + fk[1, e].astype(F32)) + (fk[2, e].astype(F32) + fk[3, e].astype(F32))
    last = pltpu.make_async_copy(fmo, om, loc.at[2])
    last.start()

    await_on(op, gr)
    here = own_ctx == ctx

    @pl.when(here)
    def _():
        await_on(op.at[pl.ds(0, 2)], gs)
        await_on(m1.at[pl.ds(0, 7)], fks)

    @pl.when(jnp.logical_not(here))
    def _():
        await_on(op, gs)
        await_on(m1.at[pl.ds(0, 8)], fks)

    @pl.when(r // 2 == y)
    def _():
        await_on(m1.at[pl.ds(0, 31)], fqs)

    @pl.when(r // 2 != y)
    def _():
        await_on(m1.at[pl.ds(0, 32)], fqs)

    await_on(xin.at[pl.ds(0, 3)], xs)
    await_on(yin.at[pl.ds(0, 3)], ys)
    await_on(m1.at[pl.ds(0, 60)], m1s)
    sent(praw, ps.at[0], pre_ctx, pre_f)
    sent(pnr, ps.at[1], pre_ctx, pre_f)
    await_on(mkp.at[:, pl.ds(0, 112), :], m2s)
    await_on(mqa.at[:, pl.ds(0, 112), :], m3s)
    await_on(mqa, loc.at[0])
    await_on(kvh.at[:, pl.ds(0, 384), :], kvs)
    await_on(gh.at[pl.ds(0, 384), :], qgs)
    await_on(lts.at[pl.ds(0, 24)], lqs)
    await_on(dl.at[pl.ds(0, 384), :], oqs)
    await_on(gkv.at[:, pl.ds(0, 384), :], kos)
    await_on(ok, kor.at[0])
    await_on(ov, kor.at[1])
    for sem in (ss, us):
        await_on(rin.at[pl.ds(0, 7)], sem)
    for sem in (bs, cs):
        await_on(rout.at[pl.ds(0, 7)], sem)
    await_on(rq.at[pl.ds(0, 7)], rqs)
    await_on(rk.at[pl.ds(0, 7)], rks)
    logs_out.wait()
    last.wait()


def close(dl, mq, k, v, m, p, oq, ok, ov, omq, omk, op):
    i = pl.program_id(0)
    lane = lax.broadcasted_iota(jnp.int32, (HD, HD), 1)
    for t in range(8):
        pair = mq[t]
        zero = jnp.zeros_like(pair)
        wide = jnp.concatenate((jnp.where(lane < FH, pair, zero), jnp.where(lane < FH, zero, pair)), axis=0)
        oq[:, 2 * t * HD : 2 * (t + 1) * HD] = mm(dl[:, t * HD : (t + 1) * HD], wide, 1, 1).astype(BF)

    ok[...] = k[...]
    ov[...] = v[...]

    @pl.when(i == 0)
    def _():
        for h in range(4):
            omq[h] = m[0, h // 2, :, FH * (h % 2) : FH * (h % 2 + 1)]
            omk[h] = m[1, h // 2, :, FH * (h % 2) : FH * (h % 2 + 1)]
        op[...] = p[...]


def shards(query_rows, key_rows, value_rows, grad_out, query_map, key_map, prefix_state, prefix_norm):
    dma = lambda *s: pltpu.SemaphoreType.DMA(s)
    vm = lambda dt, *s: pltpu.VMEM(s, dt)
    outs = pl.pallas_call(
        kernel,
        out_shape=(
            jax.ShapeDtypeStruct((128, 4096), BF),
            jax.ShapeDtypeStruct((32, 128, 128), BF),
            jax.ShapeDtypeStruct((128, 1024), BF),
            jax.ShapeDtypeStruct((128, 1024), BF),
            jax.ShapeDtypeStruct((2, 2, 16, 128), F32),
            jax.ShapeDtypeStruct((4, 16, 128), F32),
        ),
        in_specs=[pl.BlockSpec(memory_space=pl.ANY)] * 8,
        out_specs=[pl.BlockSpec(memory_space=pl.ANY)] * 6,
        scratch_shapes=[
            vm(BF, 4, 16, 64), vm(BF, 4, 16, 64), vm(F32, 4, 128), vm(BF, 4, 16, 128), vm(F32, 2, 8, 128),
            vm(BF, 64, 16, 128), vm(BF, 8, 16, 128), vm(BF, 32, 16, 128),
            vm(BF, 8, 128, 128), vm(BF, 32, 128, 128), vm(BF, 8, 128, 128),
            vm(BF, 128, 8192), vm(BF, 32, 128, 128), vm(BF, 8, 128, 512),
            vm(BF, 512, 2048), vm(BF, 2, 512, 256),
            vm(BF, 2, EXL, 512), vm(BF, 16, 512, 128), vm(BF, 16, 128, 512), vm(F32, 16, 128, 512),
            vm(BF, 16, EXL, 128), vm(BF, 16, EXL, 128),
            vm(BF, 8, 2, EXL, 128), vm(BF, 8, 2, EXL, 128),
            vm(BF, 4, 2, EXL, 128), vm(BF, 4, 2, EXL, 128), vm(F32, 2, 128, 128), vm(F32, 2, 8, 128),
            vm(BF, 8, 2, EXL, 128), vm(BF, 8, 2, EXL, 128),
            vm(BF, 16, EXL, 128), vm(BF, 16, EXL, 128),
            vm(F32, 16, 128, 512), vm(F32, 2, 128, 512), vm(F32, 2, 512, 128),
            vm(F32, 16, 128, 512), vm(BF, 16, 128, 512), vm(BF, 16, 512, 512), vm(BF, 16, 512, 512), vm(BF, 16, 128, 512), vm(F32, 16, 1, 512),
            vm(BF, 512, 1024), vm(BF, 128, 4096), vm(BF, 8, 4, 128, 128), vm(BF, 8, 4, 128, 128),
            vm(BF, 8, 128, 128), vm(BF, 8, 128, 128), vm(BF, 4, 128, 128), vm(BF, 128, 128),
            vm(BF, 4, 4, 2, 16, 128), vm(BF, 4, 2, 16, 128), vm(F32, 2, 2, 16, 128), vm(F32, 2, 128, 128),
            vm(BF, 2, 512, 256), vm(F32, 2, EXT, 128),
            dma(), dma(), dma(), dma(), dma(), dma(), dma(2), dma(2), dma(), dma(), dma(), dma(8), dma(), dma(8), dma(4),
            dma(), dma(), dma(), dma(), dma(), dma(8), dma(), dma(), dma(), dma(), dma(), dma(8), dma(), dma(8), dma(), dma(2),
            dma(), dma(), dma(), dma(), dma(), dma(), dma(), dma(), dma(), dma(),
        ],
        compiler_params=pltpu.CompilerParams(
            collective_id=0, has_side_effects=True, vmem_limit_bytes=63 * 1024 * 1024
        ),
    )(query_map, key_map, prefix_state, prefix_norm, query_rows, grad_out, key_rows, value_rows)
    log_q, map_q, grad_k, grad_v, grad_m, grad_p = outs
    whole = lambda *s: pl.BlockSpec(s, lambda i: (0,) * len(s))
    return pl.pallas_call(
        close,
        grid=(4,),
        out_shape=(
            jax.ShapeDtypeStruct((128, 8192), BF),
            jax.ShapeDtypeStruct((128, 1024), BF),
            jax.ShapeDtypeStruct((128, 1024), BF),
            jax.ShapeDtypeStruct((4, 16, 64), F32),
            jax.ShapeDtypeStruct((4, 16, 64), F32),
            jax.ShapeDtypeStruct((4, 16, 128), F32),
        ),
        in_specs=[
            pl.BlockSpec((128, 1024), lambda i: (0, i)),
            pl.BlockSpec((8, 128, 128), lambda i: (i, 0, 0)),
            pl.BlockSpec((128, 256), lambda i: (0, i)),
            pl.BlockSpec((128, 256), lambda i: (0, i)),
            whole(2, 2, 16, 128),
            whole(4, 16, 128),
        ],
        out_specs=[
            pl.BlockSpec((128, 2048), lambda i: (0, i)),
            pl.BlockSpec((128, 256), lambda i: (0, i)),
            pl.BlockSpec((128, 256), lambda i: (0, i)),
            whole(4, 16, 64),
            whole(4, 16, 64),
            whole(4, 16, 128),
        ],
    )(log_q, map_q, grad_k, grad_v, grad_m, grad_p)


def solution(mesh):
    both = ("fsdp", "ctx")
    rows = P(both, None)
    return jax.shard_map(
        shards,
        mesh=mesh,
        in_specs=(
            rows, rows, rows, rows,
            P("ctx", "fsdp", None), P("ctx", "fsdp", None),
            P("ctx", None, None), P("ctx", None),
        ),
        out_specs=(
            rows, rows, rows,
            P("ctx", "fsdp", None), P("ctx", "fsdp", None), P("ctx", "fsdp", None),
        ),
        check_vma=False,
    )
```
